128 devices in a mesh: sample: 8 (over y_hi, z), landmark: 16 (over y_lo, x, core).
Axes of the slice: x: 4, y: 4 (y_hi: 2, y_lo: 2; y = y_hi * 2 + y_lo), z: 4, core: 2. Of those that a mesh axis runs over, the one named last changes fastest.
Arguments:
- embeddings: bfloat16 [8192, 4096], P('sample'), may hold values from -6 to 6
- landmarks: bfloat16 [16384, 4096], P('landmark'), may hold values from -6 to 6
- factor: bfloat16 [16384, 16384], P('landmark', 'sample')
- flips: int32 [512, 8192], P(None, 'sample'), may hold values from 0 to 1
- labels: int32 [8192], P('sample'), may hold values from 0 to 1, as said below
- counts: int32 [8], replicated, may hold values from 256 to 1024, as said below
Outputs:
- whitened: bfloat16 [16384, 512], P(('sample', 'landmark'))
- statistic: float32 [512], replicated
The draws below stay inside these ranges and needn't reach their ends.
Inputs may be any that keep to these rules, and one draw needn't show every extreme that they name: `counts`: one slab holds exactly 1024 live rows. `labels`: 0 or 1; the first slot of every slab is of corpus 0 and the second of corpus 1.
All inputs are finite; a program needn't handle non-finite values.
Results may differ from the reference program's by a relative error of at most 0.029.
Values may be sent and summed in bfloat16 or wider, within the bound.
A program may use at most 128 MiB of HBM per device.

```python
import math
import jax
import jax.numpy as jnp
from jax import lax

D = 4096
LANDMARKS = 16384
PERMS = 512
ROWS_DEV = 1024
ROWS = 8192
N_SAMPLE = 8
N_LANDMARK = 16


def draw_factor(key, part):
    entry_key = jax.random.fold_in(key, 11)
    scale_key = jax.random.fold_in(key, 12)
    entries = jnp.clip(jax.random.normal(entry_key, (LANDMARKS, LANDMARKS), jnp.float32), -5.0, 5.0)
    logs = jax.random.uniform(scale_key, (1, LANDMARKS), jnp.float32, -1.204, 1.099)
    values = entries * jnp.exp(logs) * (1.0 / jnp.sqrt(jnp.float32(LANDMARKS)))
    return values.astype(jnp.bfloat16)


def draw_labels(key, part):
    slabs = ROWS // ROWS_DEV
    side = jax.random.randint(jax.random.fold_in(key, 22), (), 0, 2, dtype=jnp.int32)
    base = jax.random.randint(jax.random.fold_in(key, 23), (), 20, 36, dtype=jnp.int32)
    share = jnp.where(side == 0, base, 100 - base)
    jitter = jax.random.randint(jax.random.fold_in(key, 24), (slabs,), -10, 11, dtype=jnp.int32)
    threshold = share + jitter
    slab_of = jnp.arange(ROWS, dtype=jnp.int32) // ROWS_DEV
    row_threshold = jnp.sum(jnp.where(slab_of[:, None] == jnp.arange(slabs, dtype=jnp.int32)[None, :], threshold[None, :], 0), axis=1)
    draws = jax.random.randint(jax.random.fold_in(key, 21), (ROWS,), 0, 100, dtype=jnp.int32)
    bits = jnp.where(draws < row_threshold, 1, 0)
    slot = jnp.arange(ROWS, dtype=jnp.int32) % ROWS_DEV
    bits = jnp.where(slot == 0, 0, bits)
    bits = jnp.where(slot == 1, 1, bits)
    return bits.astype(jnp.int32)


def draw_counts(key, part):
    slabs = ROWS // ROWS_DEV
    base = jax.random.randint(jax.random.fold_in(key, 31), (slabs,), ROWS_DEV // 4, ROWS_DEV + 1, dtype=jnp.int32)
    chosen = jax.random.randint(jax.random.fold_in(key, 32), (), 0, slabs, dtype=jnp.int32)
    return jnp.where(jnp.arange(slabs, dtype=jnp.int32) == chosen, ROWS_DEV, base).astype(jnp.int32)


def with_ends(drawn, own_key, smallest, high):
    spot = [jax.random.randint(jax.random.fold_in(own_key, axis), (), 0, length) for axis, length in enumerate(drawn.shape)]
    main_axis = drawn.shape.index(max(drawn.shape))
    beside = spot[:main_axis] + [(spot[main_axis] + 1) % drawn.shape[main_axis]] + spot[main_axis + 1:]
    return drawn.at[tuple(spot)].set(smallest).at[tuple(beside)].set(high)


def block_scale(own_key, shape, shards, smallest, top_value):
    def one(position, shards_of):
        heights = jax.random.uniform(jax.random.fold_in(jax.random.fold_in(own_key, 6), position), (shards_of,), jnp.float32, smallest / len(shards), top_value / len(shards))
        return jnp.repeat(jnp.exp(heights), shape[position] // shards_of).reshape((-1,) + (1,) * (len(shape) - position - 1))

    level = one(*shards[0])
    for cut in shards[1:]:
        level = level * one(*cut)
    return level


def normal_values(key, dims, spread, reach, shards=(), held_as=jnp.bfloat16):
    loudness = block_scale(key, dims, shards, -0.22, 0.18) if shards else 1.0
    drawn = jax.random.normal(key, dims, jnp.float32) * spread * loudness
    return jnp.minimum(jnp.maximum(drawn, -reach), reach).astype(held_as)


def setup_inputs(seed: int = 0) -> dict:
    key_of = jax.random.split(jax.random.key(seed), 7)
    embeddings = normal_values(key_of[0], (ROWS, D), 1.0, 6.0, ((0, 8),))
    landmarks = normal_values(key_of[1], (LANDMARKS, D), 1.0, 6.0, ((0, 16),))
    factor = draw_factor(jax.random.fold_in(key_of[6], 71), 0)
    flips = with_ends(jax.random.randint(key_of[3], (PERMS, ROWS), 0, 2), jax.random.fold_in(key_of[3], 1), 0, 1).astype(jnp.int32)
    labels = draw_labels(jax.random.fold_in(key_of[6], 71), 0)
    counts = draw_counts(jax.random.fold_in(key_of[6], 71), 0)
    return {"embeddings": embeddings, "landmarks": landmarks, "factor": factor, "flips": flips, "labels": labels, "counts": counts}


def reference(embeddings, landmarks, factor, flips, labels, counts):
    total_rows = embeddings.shape[0]
    slot_index = jnp.arange(total_rows, dtype=jnp.int32)
    slab_index = slot_index // ROWS_DEV
    live_rows = (slot_index % ROWS_DEV < counts[slab_index]).astype(jnp.float32)
    corpus = labels.astype(jnp.float32)
    count_a = jnp.sum(live_rows * (1.0 - corpus))
    count_b = jnp.sum(live_rows * corpus)
    balance = jnp.sqrt(count_a * count_b / (count_a + count_b))
    row_weight = live_rows * ((1.0 - corpus) / count_a - corpus / count_b) * balance
    wide_x = embeddings.astype(jnp.float32)
    row_scale = lax.rsqrt(lax.optimization_barrier(jnp.mean(wide_x * wide_x, axis=1)) + 1e-06)
    signs = (2 * flips - 1).astype(jnp.bfloat16)
    slab_signs = signs.reshape(PERMS, N_SAMPLE, ROWS_DEV).astype(jnp.float32)
    block_size = LANDMARKS // N_LANDMARK

    def kernel_block(points):
        wide_z = points.astype(jnp.float32)
        point_scale = lax.rsqrt(lax.optimization_barrier(jnp.mean(wide_z * wide_z, axis=1)) + 1e-06)
        cross = lax.dot_general(embeddings, points, (((1,), (1,)), ((), ())), preferred_element_type=jnp.float32)
        kern = jnp.exp(0.5 * cross * row_scale[:, None] * point_scale[None, :] / math.sqrt(D))
        weighted = (row_weight[:, None] * kern).astype(jnp.bfloat16)
        slab_weighted = weighted.reshape(N_SAMPLE, ROWS_DEV, block_size).astype(jnp.float32)
        slab_moments = jnp.einsum('psr,srl->spl', slab_signs, slab_weighted).astype(jnp.bfloat16)
        slab_moments = lax.optimization_barrier(slab_moments)
        return lax.optimization_barrier(jnp.sum(slab_moments.astype(jnp.float32), axis=0)).astype(jnp.bfloat16)
    blocks = landmarks.reshape(N_LANDMARK, block_size, D)
    moments = lax.map(kernel_block, blocks)
    moments = jnp.transpose(moments, (1, 0, 2)).reshape(PERMS, LANDMARKS)
    wide = lax.dot_general(factor, moments, (((0,), (1,)), ((), ())), preferred_element_type=jnp.float32)
    statistic = lax.optimization_barrier(jnp.sum(wide * wide, axis=0)) / LANDMARKS
    return (wide.astype(jnp.bfloat16), statistic)
```

```python
import jax
import jax.numpy as jnp
from jax import lax
from jax.experimental import pallas as pl
from jax.experimental.pallas import tpu as pltpu
from jax.sharding import PartitionSpec as P

D = 4096
LANDMARKS = 16384
MESH = pl.DeviceIdType.MESH
F32 = jnp.float32
BF16 = jnp.bfloat16
CHUNK = 256
CHUNKS = 4
ROWS = 1024
BLOCK = 256
BLOCKS = ROWS // BLOCK
HALF = 32

SLABS = [(1, 2), (1, 1), (1, 3), (0, 2), (1, 0), (0, 1), (0, 3)]
CHIPS = [(1, 2), (1, 1), (1, 3), (0, 2), (1, 0), (0, 1), (0, 3)]


def kernel(
    counts_ref, labels_ref, emb_hbm, land_hbm, factor_hbm, flips_hbm,
    white_ref, stat_ref,
    emb, land, factor, flips, signs, weighted, row_scale, col_a, col_b, col_w,
    partial_buf, slab_in, own_sum, moments, acc, wide_out, wide_in, wide_rows,
    count_out, count_in, stat_out, stat_in, total_out, total_in,
    emb_sem, land_sem, factor_sem, flips_sem,
    factor_send, factor_recv, count_send, count_recv, slab_send, slab_recv,
    mom_send, mom_recv, wide_send, wide_recv, stat_send, stat_recv, total_send, total_recv,
):
    slab = lax.axis_index("sample")
    place = lax.axis_index("landmark")
    y_hi, z = slab // 4, slab % 4
    y_lo, x, core = place // 8, (place // 2) % 4, place % 2
    other = (core + 1) % 2

    def slab_at(offset):
        return ((y_hi + offset[0]) % 2) * 4 + (z + offset[1]) % 4

    def chip_at(offset):
        return ((y_lo + offset[0]) % 2) * 4 + (x + offset[1]) % 4

    def core_at(step):
        return (core + step) % 2

    here = (y_lo * 4 + x) * 2

    def emb_copy(b):
        rows = pl.ds(b * BLOCK, BLOCK)
        return pltpu.make_async_copy(emb_hbm.at[rows], emb.at[rows], emb_sem.at[b])

    def land_copy(k):
        rows = pl.ds(k * CHUNK, CHUNK)
        return pltpu.make_async_copy(land_hbm.at[rows], land.at[rows], land_sem.at[k])

    def factor_copy(k):
        return pltpu.make_async_copy(
            factor_hbm.at[pl.ds(k * CHUNK, CHUNK)],
            factor.at[k, pl.ds(core * CHUNK, CHUNK)],
            factor_sem.at[k],
        )

    def factor_share(k):
        return pltpu.make_async_remote_copy(
            src_ref=factor_hbm.at[pl.ds(k * CHUNK, CHUNK)],
            dst_ref=factor.at[k, pl.ds(core * CHUNK, CHUNK)],
            send_sem=factor_send.at[k],
            recv_sem=factor_recv.at[k],
            device_id=(slab, here + other),
            device_id_type=MESH,
        )

    flips_copy = pltpu.make_async_copy(flips_hbm, flips, flips_sem)
    land_copy(0).start()
    for b in range(BLOCKS):
        emb_copy(b).start()
    flips_copy.start()
    for k in range(1, CHUNKS):
        land_copy(k).start()

    barrier = pltpu.get_barrier_semaphore()
    friends = [(slab, here + other)]
    for offset in SLABS:
        for step in range(2):
            friends.append((slab_at(offset), here + core_at(step)))
    for offset in CHIPS:
        for step in range(2):
            friends.append((slab, chip_at(offset) * 2 + core_at(step)))
    for friend in friends:
        pl.semaphore_signal(barrier, inc=1, device_id=friend, device_id_type=MESH)

    own_count = counts_ref[slab]
    corpus = labels_ref[...].astype(F32)
    slot = lax.broadcasted_iota(jnp.int32, (8, 128), 0) * 128 + lax.broadcasted_iota(
        jnp.int32, (8, 128), 1
    )
    live = jnp.where(slot < own_count, 1.0, 0.0).astype(F32)
    in_a, in_b = live * (1.0 - corpus), live * corpus
    count_out[0] = jnp.broadcast_to(jnp.sum(in_a, keepdims=True), (8, 128))
    count_out[1] = jnp.broadcast_to(jnp.sum(in_b, keepdims=True), (8, 128))

    pl.semaphore_wait(barrier, len(friends))

    def count_copy(i):
        return pltpu.make_async_remote_copy(
            src_ref=count_out,
            dst_ref=count_in.at[i],
            send_sem=count_send.at[i],
            recv_sem=count_recv.at[i],
            device_id=(slab_at(SLABS[i]), place),
            device_id_type=MESH,
        )

    for i in range(7):
        count_copy(i).start()
    for k in range(CHUNKS):
        factor_copy(k).start()
        factor_share(k).start()

    for i in range(8):
        rows = pl.ds(i * 128, 128)
        col_a[rows, :] = jnp.transpose(jnp.broadcast_to(in_a[i : i + 1], (128, 128)))
        col_b[rows, :] = jnp.transpose(jnp.broadcast_to(in_b[i : i + 1], (128, 128)))

    def squares(ref, start, count):
        total = jnp.zeros((count, 128), F32)
        for t in range(D // 128):
            value = ref[pl.ds(start, count), pl.ds(t * 128, 128)].astype(F32)
            total = total + value * value
        return total

    def point_scale(k):
        parts = []
        for q in range(CHUNK // 128):
            total = squares(land, pl.multiple_of(k * CHUNK + q * 128, 128), 128)
            parts.append(jnp.sum(jnp.transpose(total), axis=0, keepdims=True))
        return lax.rsqrt(jnp.concatenate(parts, axis=1) * (1.0 / D) + 1e-6)

    def wide2(value):
        return jnp.concatenate([value, value], axis=1)

    fold = 0.5 / 64.0 * 1.4426950408889634

    def slab_copy(k, i):
        there = slab_at(SLABS[i])
        return pltpu.make_async_remote_copy(
            src_ref=partial_buf.at[k, pl.ds(there * 64, 64)],
            dst_ref=slab_in.at[k, i],
            send_sem=slab_send.at[k, i],
            recv_sem=slab_recv.at[k, i],
            device_id=(there, place),
            device_id_type=MESH,
        )

    def send_moments(k):
        partial_buf[k] = jnp.dot(
            signs[...], weighted[...], preferred_element_type=F32
        ).astype(BF16)
        for i in range(7):
            slab_copy(k, i).start()

    def mom_copy(k, n):
        if n < 14:
            there, step = slab_at(SLABS[n // 2]), n % 2
        else:
            there, step = slab, 1
        return pltpu.make_async_remote_copy(
            src_ref=own_sum.at[k, pl.ds(core_at(step) * HALF, HALF)],
            dst_ref=moments.at[k, core, pl.ds(slab * HALF, HALF)],
            send_sem=mom_send.at[k, n],
            recv_sem=mom_recv.at[k, n],
            device_id=(there, here + core_at(step)),
            device_id_type=MESH,
        )

    def sum_slabs(k):
        total = partial_buf[k, pl.ds(slab * 64, 64), :].astype(F32)
        for i in range(7):
            slab_copy(k, i).wait_recv()
        for i in range(7):
            total = total + slab_in[k, i].astype(F32)
        own_sum[k] = total.astype(BF16)
        for n in range(15):
            mom_copy(k, n).start()
        moments[k, core, pl.ds(slab * HALF, HALF), :] = own_sum[
            k, pl.ds(core * HALF, HALF), :
        ]

    land_copy(0).wait()
    first_scale = point_scale(0)

    def first_block(b, _):
        start = pl.multiple_of(b * BLOCK, BLOCK)
        emb_copy(b).wait()
        for q in range(BLOCK // 64):
            rows = pl.multiple_of(start + q * 64, 64)
            total = jnp.sum(squares(emb, rows, 64), axis=1, keepdims=True)
            row_scale[pl.ds(rows, 64), :] = jnp.broadcast_to(
                lax.rsqrt(total * (1.0 / D) + 1e-6) * fold, (64, 128)
            )
        cross = lax.dot_general(
            emb[pl.ds(start, BLOCK), :],
            land[0:CHUNK, :],
            (((1,), (1,)), ((), ())),
            preferred_element_type=F32,
        )
        scale = wide2(row_scale[pl.ds(start, BLOCK), :])

        @pl.when(b == 0)
        def _():
            for i in range(7):
                count_copy(i).wait()
            count_a, count_b = count_out[0], count_out[1]
            for i in range(7):
                count_a = count_a + count_in[i, 0]
                count_b = count_b + count_in[i, 1]
            balance = jnp.sqrt(count_a * count_b / (count_a + count_b))
            gain_a = (balance / count_a)[0:1]
            gain_b = (balance / count_b)[0:1]
            col_w[...] = col_a[...] * gain_a - col_b[...] * gain_b

        weight = wide2(col_w[pl.ds(start, BLOCK), :])
        weighted[pl.ds(start, BLOCK), :] = (
            jnp.exp2(cross * scale * first_scale) * weight
        ).astype(BF16)
        return 0

    lax.fori_loop(0, BLOCKS, first_block, 0)
    flips_copy.wait()
    signs[...] = (2 * flips[...] - 1).astype(F32).astype(BF16)
    send_moments(0)

    def later_chunk(k, _):
        land_copy(k).wait()
        points = point_scale(k)
        cross = lax.dot_general(
            emb[...],
            land[pl.ds(pl.multiple_of(k * CHUNK, CHUNK), CHUNK), :],
            (((1,), (1,)), ((), ())),
            preferred_element_type=F32,
        )
        weighted[...] = (
            jnp.exp2(cross * wide2(row_scale[...]) * points) * wide2(col_w[...])
        ).astype(BF16)
        send_moments(k)

        @pl.when(k >= 2)
        def _():
            sum_slabs(k - 2)

        return 0

    lax.fori_loop(1, CHUNKS, later_chunk, 0)

    def moments_of(k):
        for n in range(15):
            mom_copy(k, n).wait_recv()
        return jnp.concatenate([moments[k, 0], moments[k, 1]], axis=1)

    def whiten(k):
        left = moments_of(k)

        def tile(q, _):
            value = jnp.dot(
                left,
                factor[k, :, pl.ds(pl.multiple_of(q * 256, 256), 256)],
                preferred_element_type=F32,
            )
            if k == 0:
                acc[q] = value
            else:
                acc[q] = acc[q] + value
            return 0

        lax.fori_loop(0, 8, tile, 0)

    sum_slabs(CHUNKS - 2)
    for k in range(CHUNKS):
        factor_copy(k).wait()
        factor_share(k).wait()
    whiten(0)
    sum_slabs(CHUNKS - 1)
    for k in range(1, CHUNKS - 1):
        whiten(k)

    def wide_copy(t, step):
        chip = chip_at(CHIPS[t]) if t < 7 else y_lo * 4 + x
        return pltpu.make_async_remote_copy(
            src_ref=wide_out.at[t, core_at(step)],
            dst_ref=wide_in.at[t, core],
            send_sem=wide_send.at[t, step],
            recv_sem=wide_recv.at[t, step],
            device_id=(slab, chip * 2 + core_at(step)),
            device_id_type=MESH,
        )

    last = CHUNKS - 1
    left = moments_of(last)
    for t in range(8):
        q = chip_at(CHIPS[t]) if t < 7 else y_lo * 4 + x
        value = acc[q] + jnp.dot(
            left,
            factor[last, :, pl.ds(pl.multiple_of(q * 256, 256), 256)],
            preferred_element_type=F32,
        )
        value = value.astype(BF16)
        wide_out[t, 0] = value[:, :128]
        wide_out[t, 1] = value[:, 128:]
        if t < 7:
            wide_copy(t, 0).start()
        wide_copy(t, 1).start()
    wide_in[7, core] = wide_out[7, core]

    for t in range(8):
        if t < 7:
            wide_copy(t, 0).wait_recv()
        wide_copy(t, 1).wait_recv()
    for c in range(2):
        total = wide_in[0, c].astype(F32)
        for t in range(1, 8):
            total = total + wide_in[t, c].astype(F32)
        for s in range(8):
            wide_rows[pl.ds(s * 64 + c * HALF, HALF), :] = total[s * HALF : (s + 1) * HALF]
    stat_out[...] = jnp.zeros((8, 128), F32)
    for i in range(4):
        turned = jnp.transpose(wide_rows[pl.ds(i * 128, 128), :])
        white_ref[:, pl.ds(i * 128, 128)] = turned.astype(BF16)
        stat_out[pl.ds(i, 1), :] = jnp.sum(turned * turned, axis=0, keepdims=True)

    def stat_copy(n):
        if n < 14:
            there, step = chip_at(CHIPS[n // 2]), n % 2
        else:
            there, step = y_lo * 4 + x, 1
        return pltpu.make_async_remote_copy(
            src_ref=stat_out,
            dst_ref=stat_in.at[place],
            send_sem=stat_send.at[n],
            recv_sem=stat_recv.at[n],
            device_id=(slab, there * 2 + core_at(step)),
            device_id_type=MESH,
        )

    for n in range(15):
        stat_copy(n).start()
    stat_in[place] = stat_out[...]
    for n in range(15):
        stat_copy(n).wait_recv()
    total = stat_in[0]
    for n in range(1, 16):
        total = total + stat_in[n]
    total_out[...] = total

    def total_copy(i):
        return pltpu.make_async_remote_copy(
            src_ref=total_out,
            dst_ref=total_in.at[slab],
            send_sem=total_send.at[i],
            recv_sem=total_recv.at[i],
            device_id=(slab_at(SLABS[i]), place),
            device_id_type=MESH,
        )

    for i in range(7):
        total_copy(i).start()
    total_in[slab] = total_out[...]

    for k in range(CHUNKS):
        for i in range(7):
            slab_copy(k, i).wait_send()
        for n in range(15):
            mom_copy(k, n).wait_send()
    for t in range(8):
        if t < 7:
            wide_copy(t, 0).wait_send()
        wide_copy(t, 1).wait_send()
    for n in range(15):
        stat_copy(n).wait_send()

    for i in range(7):
        total_copy(i).wait()
    total = total_in[0]
    for i in range(1, 8):
        total = total + total_in[i]
    stat_ref[...] = total[0:4] * (1.0 / LANDMARKS)


def local(embeddings, landmarks, factor, flips, labels, counts):
    any_space = pl.BlockSpec(memory_space=pl.ANY)
    vmem = pl.BlockSpec(memory_space=pltpu.VMEM)
    dma = pltpu.SemaphoreType.DMA
    whitened, statistic = pl.pallas_call(
        kernel,
        out_shape=(
            jax.ShapeDtypeStruct((128, 512), BF16),
            jax.ShapeDtypeStruct((4, 128), F32),
        ),
        in_specs=[pl.BlockSpec(memory_space=pltpu.SMEM), vmem] + [any_space] * 4,
        out_specs=(vmem, vmem),
        scratch_shapes=[
            pltpu.VMEM((ROWS, D), BF16),
            pltpu.VMEM((CHUNK * CHUNKS, D), BF16),
            pltpu.VMEM((CHUNKS, 2 * CHUNK, 2048), BF16),
            pltpu.VMEM((512, ROWS), jnp.int32),
            pltpu.VMEM((512, ROWS), BF16),
            pltpu.VMEM((ROWS, CHUNK), BF16),
            pltpu.VMEM((ROWS, 128), F32),
            pltpu.VMEM((ROWS, 128), F32),
            pltpu.VMEM((ROWS, 128), F32),
            pltpu.VMEM((ROWS, 128), F32),
            pltpu.VMEM((CHUNKS, 512, CHUNK), BF16),
            pltpu.VMEM((CHUNKS, 7, 64, CHUNK), BF16),
            pltpu.VMEM((CHUNKS, 64, CHUNK), BF16),
            pltpu.VMEM((CHUNKS, 2, 256, CHUNK), BF16),
            pltpu.VMEM((8, 256, 256), F32),
            pltpu.VMEM((8, 2, 256, 128), BF16),
            pltpu.VMEM((8, 2, 256, 128), BF16),
            pltpu.VMEM((512, 128), F32),
            pltpu.VMEM((2, 8, 128), F32),
            pltpu.VMEM((7, 2, 8, 128), F32),
            pltpu.VMEM((8, 128), F32),
            pltpu.VMEM((16, 8, 128), F32),
            pltpu.VMEM((8, 128), F32),
            pltpu.VMEM((8, 8, 128), F32),
            dma((BLOCKS,)),
            dma((CHUNKS,)),
            dma((CHUNKS,)),
            dma,
            dma((CHUNKS,)),
            dma((CHUNKS,)),
            dma((7,)),
            dma((7,)),
            dma((CHUNKS, 7)),
            dma((CHUNKS, 7)),
            dma((CHUNKS, 15)),
            dma((CHUNKS, 15)),
            dma((8, 2)),
            dma((8, 2)),
            dma((15,)),
            dma((15,)),
            dma((7,)),
            dma((7,)),
        ],
        compiler_params=pltpu.CompilerParams(
            collective_id=0, has_side_effects=True, vmem_limit_bytes=60 << 20
        ),
    )(counts, labels.reshape(8, 128), embeddings, landmarks, factor, flips)
    return whitened, statistic.reshape(512)


def solution(mesh):
    return jax.shard_map(
        local,
        mesh=mesh,
        in_specs=(
            P("sample", None),
            P("landmark", None),
            P("landmark", "sample"),
            P(None, "sample"),
            P("sample"),
            P(),
        ),
        out_specs=(P(("sample", "landmark"), None), P()),
        check_vma=False,
    )
```

```python
import jax
import jax.numpy as jnp
from jax import lax
from jax.experimental import pallas as pl
from jax.experimental.pallas import tpu as pltpu
from jax.sharding import PartitionSpec as P

D = 4096
LANDMARKS = 16384
MESH = pl.DeviceIdType.MESH
F32 = jnp.float32
BF16 = jnp.bfloat16
CHUNK = 256
CHUNKS = 4
ROWS = 1024
BLOCK = 256
BLOCKS = ROWS // BLOCK
PART = 16

SLABS = [(1, 2), (1, 1), (1, 3), (0, 2), (1, 0), (0, 1), (0, 3)]
CHIPS = [(1, 2), (1, 1), (1, 3), (0, 2), (1, 0), (0, 1), (0, 3)]


def kernel(
    counts_ref, labels_ref, emb_hbm, land_hbm, factor_hbm, flips_hbm,
    white_ref, stat_ref,
    emb, land, factor, flips, signs, weighted, row_scale, col_a, col_b, col_w, kern,
    partial_buf, slab_in, own_sum, moments, wide_out, wide_in, wide_rows,
    count_out, count_in, stat_out, stat_in, total_out, total_in,
    emb_sem, land_sem, factor_sem, flips_sem,
    factor_send, factor_recv, count_send, count_recv, slab_send, slab_recv,
    early_send, early_recv, late_send, late_recv, wide_send, wide_recv, stat_send, stat_recv, total_send, total_recv,
):
    slab = lax.axis_index("sample")
    place = lax.axis_index("landmark")
    y_hi, z = slab // 4, slab % 4
    y_lo, x, core = place // 8, (place // 2) % 4, place % 2
    other = (core + 1) % 2

    def slab_at(offset):
        return ((y_hi + offset[0]) % 2) * 4 + (z + offset[1]) % 4

    def chip_at(offset):
        return ((y_lo + offset[0]) % 2) * 4 + (x + offset[1]) % 4

    def core_at(step):
        return (core + step) % 2

    here = (y_lo * 4 + x) * 2

    def settle(like, sem):
        pltpu.make_async_copy(like, like, sem).wait()

    def emb_copy(b):
        rows = pl.ds(b * BLOCK, BLOCK)
        return pltpu.make_async_copy(emb_hbm.at[rows], emb.at[rows], emb_sem.at[b])

    def land_copy(k):
        rows = pl.ds(k * CHUNK, CHUNK)
        return pltpu.make_async_copy(land_hbm.at[rows], land.at[rows], land_sem.at[k])

    def factor_copy(k):
        return pltpu.make_async_copy(
            factor_hbm.at[pl.ds(k * CHUNK, CHUNK)],
            factor.at[core, pl.ds(k * CHUNK, CHUNK)],
            factor_sem,
        )

    def factor_share(k):
        return pltpu.make_async_remote_copy(
            src_ref=factor_hbm.at[pl.ds(k * CHUNK, CHUNK)],
            dst_ref=factor.at[core, pl.ds(k * CHUNK, CHUNK)],
            send_sem=factor_send,
            recv_sem=factor_recv,
            device_id=(slab, here + other),
            device_id_type=MESH,
        )

    flips_copy = pltpu.make_async_copy(flips_hbm, flips, flips_sem)
    land_copy(0).start()
    for b in range(BLOCKS):
        emb_copy(b).start()

    barrier = pltpu.get_barrier_semaphore()
    friends = [(slab, here + other)]
    for offset in SLABS:
        for step in range(2):
            friends.append((slab_at(offset), here + core_at(step)))
    for offset in CHIPS:
        for step in range(2):
            friends.append((slab, chip_at(offset) * 2 + core_at(step)))
    for friend in friends:
        pl.semaphore_signal(barrier, inc=1, device_id=friend, device_id_type=MESH)

    own_count = counts_ref[slab]
    corpus = labels_ref[...].astype(F32)
    slot = lax.broadcasted_iota(jnp.int32, (8, 128), 0) * 128 + lax.broadcasted_iota(
        jnp.int32, (8, 128), 1
    )
    live = jnp.where(slot < own_count, 1.0, 0.0).astype(F32)
    in_a, in_b = live * (1.0 - corpus), live * corpus
    count_out[0] = jnp.broadcast_to(jnp.sum(in_a, keepdims=True), (8, 128))
    count_out[1] = jnp.broadcast_to(jnp.sum(in_b, keepdims=True), (8, 128))

    def squares(ref, start, count):
        total = jnp.zeros((count, 128), F32)
        for t in range(D // 128):
            value = ref[pl.ds(start, count), pl.ds(t * 128, 128)].astype(F32)
            total = total + value * value
        return total

    def lane_sums(value):
        return lax.dot_general(
            jnp.ones((8, 128), F32),
            value,
            (((1,), (1,)), ((), ())),
            precision=lax.Precision.HIGHEST,
            preferred_element_type=F32,
        )

    def point_scale(k):
        parts = []
        for q in range(CHUNK // 64):
            parts.append(squares(land, pl.multiple_of(k * CHUNK + q * 64, 64), 64))
        total = lane_sums(jnp.concatenate(parts, axis=0))
        return lax.rsqrt(total[0:1] * (1.0 / D) + 1e-6)

    def wide2(value):
        return jnp.concatenate([value, value], axis=1)

    fold = 0.5 / 64.0 * 1.4426950408889634

    def slab_copy(k, i):
        there = slab_at(SLABS[i])
        return pltpu.make_async_remote_copy(
            src_ref=partial_buf.at[k, pl.ds(there * 64, 64)],
            dst_ref=slab_in.at[k, i],
            send_sem=slab_send,
            recv_sem=slab_recv.at[k],
            device_id=(there, place),
            device_id_type=MESH,
        )

    def send_moments(k):
        partial_buf[k] = jnp.dot(
            signs[...], weighted[...], preferred_element_type=F32
        ).astype(BF16)
        for i in range(7):
            slab_copy(k, i).start()

    def mom_target(n):
        if n < 14:
            return slab_at(SLABS[n // 2]), n % 2
        return slab, 1

    def early_copy(k, n):
        there, step = mom_target(n)
        columns = pl.ds(k * CHUNK, CHUNK)
        return pltpu.make_async_remote_copy(
            src_ref=own_sum.at[0, core_at(step), :, columns],
            dst_ref=moments.at[0, core * 8 + slab, :, columns],
            send_sem=early_send,
            recv_sem=early_recv,
            device_id=(there, here + core_at(step)),
            device_id_type=MESH,
        )

    def late_copy(n):
        there, step = mom_target(n)
        return pltpu.make_async_remote_copy(
            src_ref=own_sum.at[1, core_at(step)],
            dst_ref=moments.at[1, core * 8 + slab],
            send_sem=late_send,
            recv_sem=late_recv,
            device_id=(there, here + core_at(step)),
            device_id_type=MESH,
        )

    def sum_slabs(k):
        total = partial_buf[k, pl.ds(slab * 64, 64), :].astype(F32)
        settle(slab_in.at[k], slab_recv.at[k])
        for i in range(7):
            total = total + slab_in[k, i].astype(F32)
        total = total.astype(BF16)
        columns = pl.ds(pl.multiple_of(k * CHUNK, CHUNK), CHUNK)
        for c in range(2):
            for h in range(2):
                start = (2 * c + h) * PART
                own_sum[h, c, :, columns] = total[start : start + PART]
        for n in range(15):
            early_copy(k, n).start()

    land_copy(0).wait()
    first_scale = point_scale(0)

    def first_block(b, _):
        start = pl.multiple_of(b * BLOCK, BLOCK)
        emb_copy(b).wait()
        for q in range(BLOCK // 64):
            rows = pl.multiple_of(start + q * 64, 64)
            total = jnp.sum(squares(emb, rows, 64), axis=1, keepdims=True)
            row_scale[pl.ds(rows, 64), :] = jnp.broadcast_to(
                lax.rsqrt(total * (1.0 / D) + 1e-6) * fold, (64, 128)
            )
        cross = lax.dot_general(
            emb[pl.ds(start, BLOCK), :],
            land[0:CHUNK, :],
            (((1,), (1,)), ((), ())),
            preferred_element_type=F32,
        )
        scale = wide2(row_scale[pl.ds(start, BLOCK), :])
        kern[pl.ds(start, BLOCK), :] = jnp.exp2(cross * scale * first_scale)
        return 0

    first_block(0, 0)
    pl.semaphore_wait(barrier, len(friends))

    def count_copy(i):
        return pltpu.make_async_remote_copy(
            src_ref=count_out,
            dst_ref=count_in.at[i],
            send_sem=count_send,
            recv_sem=count_recv,
            device_id=(slab_at(SLABS[i]), place),
            device_id_type=MESH,
        )

    for i in range(7):
        count_copy(i).start()
    flips_copy.start()
    for k in range(1, CHUNKS):
        land_copy(k).start()
    lax.fori_loop(1, BLOCKS, first_block, 0)

    eye = lax.broadcasted_iota(jnp.int32, (128, 128), 0) == lax.broadcasted_iota(
        jnp.int32, (128, 128), 1
    )
    for row, column in ((in_a, col_a), (in_b, col_b)):
        for i in range(8):
            spread = jnp.where(eye, jnp.broadcast_to(row[i : i + 1], (128, 128)), 0.0)
            column[pl.ds(i * 128, 128), :] = jnp.dot(
                spread.astype(BF16), jnp.ones((128, 128), BF16), preferred_element_type=F32
            )
    flips_copy.wait()
    signs[...] = (2 * flips[...] - 1).astype(F32).astype(BF16)
    settle(count_in, count_send)
    settle(count_in, count_recv)
    count_a, count_b = count_out[0], count_out[1]
    for i in range(7):
        count_a = count_a + count_in[i, 0]
        count_b = count_b + count_in[i, 1]
    balance = jnp.sqrt(count_a * count_b / (count_a + count_b))
    gain_a = (balance / count_a)[0:1]
    gain_b = (balance / count_b)[0:1]
    col_w[...] = col_a[...] * gain_a - col_b[...] * gain_b
    weighted[...] = (kern[...] * wide2(col_w[...])).astype(BF16)
    send_moments(0)
    for k in range(CHUNKS):
        factor_copy(k).start()
        factor_share(k).start()

    def later_chunk(k, _):
        land_copy(k).wait()
        points = point_scale(k)
        cross = lax.dot_general(
            emb[...],
            land[pl.ds(pl.multiple_of(k * CHUNK, CHUNK), CHUNK), :],
            (((1,), (1,)), ((), ())),
            preferred_element_type=F32,
        )
        weighted[...] = (
            jnp.exp2(cross * wide2(row_scale[...]) * points) * wide2(col_w[...])
        ).astype(BF16)
        send_moments(k)

        @pl.when(k >= 2)
        def _():
            sum_slabs(k - 2)

        return 0

    lax.fori_loop(1, CHUNKS, later_chunk, 0)

    sum_slabs(CHUNKS - 2)
    sum_slabs(CHUNKS - 1)
    for n in range(15):
        late_copy(n).start()
    for h in range(2):
        moments[h, core * 8 + slab] = own_sum[h, core]
    settle(factor.at[core], factor_sem)
    settle(factor.at[core], factor_send)
    settle(factor.at[other], factor_recv)

    def wide_copy(h, t, step):
        chip = chip_at(CHIPS[t]) if t < 7 else y_lo * 4 + x
        return pltpu.make_async_remote_copy(
            src_ref=wide_out.at[h, t, core_at(step)],
            dst_ref=wide_in.at[h, core * 8 + t],
            send_sem=wide_send,
            recv_sem=wide_recv.at[h],
            device_id=(slab, chip * 2 + core_at(step)),
            device_id_type=MESH,
        )

    def whiten(h):
        left = jnp.concatenate(
            [moments[h, c * 8 : c * 8 + 8].reshape(8 * PART, ROWS) for c in range(2)], axis=1
        )
        for t in range(8):
            q = chip_at(CHIPS[t]) if t < 7 else y_lo * 4 + x
            columns = pl.ds(pl.multiple_of(q * 256, 256), 256)
            value = jnp.dot(
                left,
                jnp.concatenate([factor[0, :, columns], factor[1, :, columns]], axis=0),
                preferred_element_type=F32,
            ).astype(BF16)
            wide_out[h, t, 0] = value[:, :128]
            wide_out[h, t, 1] = value[:, 128:]
            if t < 7:
                wide_copy(h, t, 0).start()
            wide_copy(h, t, 1).start()
        wide_in[h, core * 8 + 7] = wide_out[h, 7, core]

    def gather(h):
        settle(wide_in.at[h, pl.ds(0, 15)], wide_recv.at[h])
        for c in range(2):
            total = wide_in[h, c * 8].astype(F32)
            for t in range(1, 8):
                total = total + wide_in[h, c * 8 + t].astype(F32)
            for s in range(8):
                wide_rows[pl.ds(s * 64 + c * 32 + h * PART, PART), :] = total[
                    s * PART : (s + 1) * PART
                ]

    settle(moments.at[0, pl.ds(0, 15)], early_recv)
    whiten(0)
    settle(moments.at[1, pl.ds(0, 15)], late_recv)
    whiten(1)
    gather(0)
    gather(1)
    values = wide_rows[...]
    norms = lane_sums(values * values)[0:1]
    for i in range(4):
        stat_out[pl.ds(i, 1), :] = norms[:, i * 128 : (i + 1) * 128]
    stat_out[pl.ds(4, 4), :] = jnp.zeros((4, 128), F32)

    def stat_copy(n):
        if n < 14:
            there, step = chip_at(CHIPS[n // 2]), n % 2
        else:
            there, step = y_lo * 4 + x, 1
        return pltpu.make_async_remote_copy(
            src_ref=stat_out,
            dst_ref=stat_in.at[place],
            send_sem=stat_send,
            recv_sem=stat_recv,
            device_id=(slab, there * 2 + core_at(step)),
            device_id_type=MESH,
        )

    for n in range(15):
        stat_copy(n).start()
    stat_in[place] = stat_out[...]
    for i in range(4):
        white_ref[:, pl.ds(i * 128, 128)] = jnp.transpose(
            wide_rows[pl.ds(i * 128, 128), :]
        ).astype(BF16)
    settle(stat_in.at[pl.ds(0, 15)], stat_recv)
    total = stat_in[0]
    for n in range(1, 16):
        total = total + stat_in[n]
    total_out[...] = total

    def total_copy(i):
        return pltpu.make_async_remote_copy(
            src_ref=total_out,
            dst_ref=total_in.at[slab],
            send_sem=total_send,
            recv_sem=total_recv,
            device_id=(slab_at(SLABS[i]), place),
            device_id_type=MESH,
        )

    for i in range(7):
        total_copy(i).start()
    total_in[slab] = total_out[...]

    settle(slab_in, slab_send)
    settle(moments.at[0, pl.ds(0, 15)], early_send)
    settle(moments.at[1, pl.ds(0, 15)], late_send)
    settle(wide_in.at[:, pl.ds(0, 15)], wide_send)
    settle(stat_in.at[pl.ds(0, 15)], stat_send)

    settle(total_in.at[pl.ds(0, 7)], total_send)
    settle(total_in.at[pl.ds(0, 7)], total_recv)
    total = total_in[0]
    for i in range(1, 8):
        total = total + total_in[i]
    stat_ref[...] = total


def finish(white_in, stat_in, white_ref, stat_ref):
    white_ref[...] = white_in[...]
    stat_ref[...] = stat_in[0:4] * (1.0 / LANDMARKS)


def local(embeddings, landmarks, factor, flips, labels, counts):
    any_space = pl.BlockSpec(memory_space=pl.ANY)
    vmem = pl.BlockSpec(memory_space=pltpu.VMEM)
    dma = pltpu.SemaphoreType.DMA
    whitened, statistic = pl.pallas_call(
        kernel,
        out_shape=(
            jax.ShapeDtypeStruct((128, 512), BF16),
            jax.ShapeDtypeStruct((8, 128), F32),
        ),
        in_specs=[pl.BlockSpec(memory_space=pltpu.SMEM), vmem] + [any_space] * 4,
        out_specs=(vmem, vmem),
        scratch_shapes=[
            pltpu.VMEM((ROWS, D), BF16),
            pltpu.VMEM((CHUNK * CHUNKS, D), BF16),
            pltpu.VMEM((2, ROWS, 2048), BF16),
            pltpu.VMEM((512, ROWS), jnp.int32),
            pltpu.VMEM((512, ROWS), BF16),
            pltpu.VMEM((ROWS, CHUNK), BF16),
            pltpu.VMEM((ROWS, 128), F32),
            pltpu.VMEM((ROWS, 128), F32),
            pltpu.VMEM((ROWS, 128), F32),
            pltpu.VMEM((ROWS, 128), F32),
            pltpu.VMEM((ROWS, CHUNK), F32),
            pltpu.VMEM((CHUNKS, 512, CHUNK), BF16),
            pltpu.VMEM((CHUNKS, 7, 64, CHUNK), BF16),
            pltpu.VMEM((2, 2, PART, ROWS), BF16),
            pltpu.VMEM((2, 16, PART, ROWS), BF16),
            pltpu.VMEM((2, 8, 2, 8 * PART, 128), BF16),
            pltpu.VMEM((2, 16, 8 * PART, 128), BF16),
            pltpu.VMEM((512, 128), F32),
            pltpu.VMEM((2, 8, 128), F32),
            pltpu.VMEM((7, 2, 8, 128), F32),
            pltpu.VMEM((8, 128), F32),
            pltpu.VMEM((16, 8, 128), F32),
            pltpu.VMEM((8, 128), F32),
            pltpu.VMEM((8, 8, 128), F32),
            dma((BLOCKS,)),
            dma((CHUNKS,)),
            dma,
            dma,
            dma,
            dma,
            dma,
            dma,
            dma,
            dma((CHUNKS,)),
            dma,
            dma,
            dma,
            dma,
            dma,
            dma((2,)),
            dma,
            dma,
            dma,
            dma,
        ],
        compiler_params=pltpu.CompilerParams(
            collective_id=0, has_side_effects=True, vmem_limit_bytes=60 << 20
        ),
    )(counts, labels.reshape(8, 128), embeddings, landmarks, factor, flips)
    whitened, statistic = pl.pallas_call(
        finish,
        out_shape=(
            jax.ShapeDtypeStruct((128, 512), BF16),
            jax.ShapeDtypeStruct((4, 128), F32),
        ),
        in_specs=[vmem, vmem],
        out_specs=(vmem, vmem),
    )(whitened, statistic)
    return whitened, statistic.reshape(512)


def solution(mesh):
    return jax.shard_map(
        local,
        mesh=mesh,
        in_specs=(
            P("sample", None),
            P("landmark", None),
            P("landmark", "sample"),
            P(None, "sample"),
            P("sample"),
            P(),
        ),
        out_specs=(P(("sample", "landmark"), None), P()),
        check_vma=False,
    )
```

```python
import jax
import jax.numpy as jnp
from jax import lax
from jax.experimental import pallas as pl
from jax.experimental.pallas import tpu as pltpu
from jax.sharding import PartitionSpec as P

D = 4096
LANDMARKS = 16384
MESH = pl.DeviceIdType.MESH
F32 = jnp.float32
BF16 = jnp.bfloat16
CHUNK = 256
CHUNKS = 4
ROWS = 1024
BLOCK = 256
BLOCKS = ROWS // BLOCK
PART = 16
STEPS = [2, 1, 3, 0]

SLABS = [(1, 2), (1, 1), (1, 3), (0, 2), (1, 0), (0, 1), (0, 3)]
CHIPS = [(1, 2), (1, 1), (1, 3), (0, 2), (1, 0), (0, 1), (0, 3)]
AROUND = [(a, b) for a in SLABS + [(0, 0)] for b in CHIPS + [(0, 0)]][:63]


def kernel(
    counts_ref, labels_ref, emb_hbm, land_hbm, factor_hbm, flips_hbm,
    white_ref, stat_ref,
    emb, land, factor, flips, signs, weighted, row_scale, col_a, col_b, col_w, kern,
    partial_buf, slab_in, own_sum, moments, wide_out, wide_in,
    line_out, line_in, line_own, hop_out, hop_in, wide_rows,
    count_out, count_in, stat_out, stat_in, total_in,
    emb_sem, land_sem, factor_sem, flips_sem,
    factor_send, factor_recv, count_send, count_recv, slab_send, slab_recv,
    early_send, early_recv, late_send, late_recv, wide_send, wide_recv,
    line_send, line_recv, hop_send, hop_recv, stat_send, stat_recv, total_send, total_recv,
):
    slab = lax.axis_index("sample")
    place = lax.axis_index("landmark")
    y_hi, z = slab // 4, slab % 4
    y_lo, x, core = place // 8, (place // 2) % 4, place % 2
    other = (core + 1) % 2

    def slab_at(offset):
        return ((y_hi + offset[0]) % 2) * 4 + (z + offset[1]) % 4

    def chip_at(offset):
        return ((y_lo + offset[0]) % 2) * 4 + (x + offset[1]) % 4

    def core_at(step):
        return (core + step) % 2

    here = (y_lo * 4 + x) * 2

    def settle(like, sem):
        pltpu.make_async_copy(like, like, sem).wait()

    def emb_copy(b):
        rows = pl.ds(b * BLOCK, BLOCK)
        return pltpu.make_async_copy(emb_hbm.at[rows], emb.at[rows], emb_sem.at[b])

    def land_copy(k):
        rows = pl.ds(k * CHUNK, CHUNK)
        return pltpu.make_async_copy(land_hbm.at[rows], land.at[rows], land_sem.at[k])

    def factor_copy(k):
        return pltpu.make_async_copy(
            factor_hbm.at[pl.ds(k * CHUNK, CHUNK)],
            factor.at[core, pl.ds(k * CHUNK, CHUNK)],
            factor_sem,
        )

    def factor_share(k):
        return pltpu.make_async_remote_copy(
            src_ref=factor_hbm.at[pl.ds(k * CHUNK, CHUNK)],
            dst_ref=factor.at[core, pl.ds(k * CHUNK, CHUNK)],
            send_sem=factor_send,
            recv_sem=factor_recv,
            device_id=(slab, here + other),
            device_id_type=MESH,
        )

    flips_copy = pltpu.make_async_copy(flips_hbm, flips, flips_sem)
    land_copy(0).start()
    for b in range(BLOCKS):
        emb_copy(b).start()

    barrier = pltpu.get_barrier_semaphore()
    friends = [(slab, here + other)]
    for offset in SLABS:
        for step in range(2):
            friends.append((slab_at(offset), here + core_at(step)))
    for offset in CHIPS:
        friends.append((slab, chip_at(offset) * 2 + other))
    for offset in AROUND:
        if offset[1] != (0, 0):
            friends.append((slab_at(offset[0]), chip_at(offset[1]) * 2 + core))
    for friend in friends:
        pl.semaphore_signal(barrier, inc=1, device_id=friend, device_id_type=MESH)

    own_count = counts_ref[slab]
    corpus = labels_ref[...].astype(F32)
    slot = lax.broadcasted_iota(jnp.int32, (8, 128), 0) * 128 + lax.broadcasted_iota(
        jnp.int32, (8, 128), 1
    )
    live = jnp.where(slot < own_count, 1.0, 0.0).astype(F32)
    in_a, in_b = live * (1.0 - corpus), live * corpus
    count_out[0] = jnp.broadcast_to(jnp.sum(in_a, keepdims=True), (8, 128))
    count_out[1] = jnp.broadcast_to(jnp.sum(in_b, keepdims=True), (8, 128))

    def squares(ref, start, count):
        total = jnp.zeros((count, 128), F32)
        for t in range(D // 128):
            value = ref[pl.ds(start, count), pl.ds(t * 128, 128)].astype(F32)
            total = total + value * value
        return total

    def lane_sums(value):
        return lax.dot_general(
            jnp.ones((8, 128), F32),
            value,
            (((1,), (1,)), ((), ())),
            precision=lax.Precision.HIGHEST,
            preferred_element_type=F32,
        )

    def point_scale(k):
        parts = []
        for q in range(CHUNK // 64):
            parts.append(squares(land, pl.multiple_of(k * CHUNK + q * 64, 64), 64))
        total = lane_sums(jnp.concatenate(parts, axis=0))
        return lax.rsqrt(total[0:1] * (1.0 / D) + 1e-6)

    def wide2(value):
        return jnp.concatenate([value, value], axis=1)

    fold = 0.5 / 64.0 * 1.4426950408889634

    def slab_copy(k, i):
        there = slab_at(SLABS[i])
        return pltpu.make_async_remote_copy(
            src_ref=partial_buf.at[k, pl.ds(there * 64, 64)],
            dst_ref=slab_in.at[k, i],
            send_sem=slab_send,
            recv_sem=slab_recv.at[k],
            device_id=(there, place),
            device_id_type=MESH,
        )

    def send_moments(k):
        partial_buf[k] = jnp.dot(
            signs[...], weighted[...], preferred_element_type=F32
        ).astype(BF16)
        for i in range(7):
            slab_copy(k, i).start()

    def mom_target(n):
        if n < 14:
            return slab_at(SLABS[n // 2]), n % 2
        return slab, 1

    def early_copy(k, n):
        there, step = mom_target(n)
        columns = pl.ds(k * CHUNK, CHUNK)
        return pltpu.make_async_remote_copy(
            src_ref=own_sum.at[0, core_at(step), :, columns],
            dst_ref=moments.at[0, core * 8 + slab, :, columns],
            send_sem=early_send,
            recv_sem=early_recv,
            device_id=(there, here + core_at(step)),
            device_id_type=MESH,
        )

    def late_copy(n):
        there, step = mom_target(n)
        return pltpu.make_async_remote_copy(
            src_ref=own_sum.at[1, core_at(step)],
            dst_ref=moments.at[1, core * 8 + slab],
            send_sem=late_send,
            recv_sem=late_recv,
            device_id=(there, here + core_at(step)),
            device_id_type=MESH,
        )

    def sum_slabs(k):
        total = partial_buf[k, pl.ds(slab * 64, 64), :].astype(F32)
        settle(slab_in.at[k], slab_recv.at[k])
        for i in range(7):
            total = total + slab_in[k, i].astype(F32)
        total = total.astype(BF16)
        columns = pl.ds(pl.multiple_of(k * CHUNK, CHUNK), CHUNK)
        for c in range(2):
            for h in range(2):
                start = (2 * c + h) * PART
                own_sum[h, c, :, columns] = total[start : start + PART]
        for n in range(15):
            early_copy(k, n).start()

    land_copy(0).wait()
    first_scale = point_scale(0)

    def first_rows(start, count):
        for b in range(start // BLOCK, (start + count) // BLOCK):
            emb_copy(b).wait()
        for q in range(count // 64):
            rows = start + q * 64
            total = jnp.sum(squares(emb, rows, 64), axis=1, keepdims=True)
            row_scale[pl.ds(rows, 64), :] = jnp.broadcast_to(
                lax.rsqrt(total * (1.0 / D) + 1e-6) * fold, (64, 128)
            )
        cross = lax.dot_general(
            emb[pl.ds(start, count), :],
            land[0:CHUNK, :],
            (((1,), (1,)), ((), ())),
            preferred_element_type=F32,
        )
        scale = wide2(row_scale[pl.ds(start, count), :])
        kern[pl.ds(start, count), :] = jnp.exp2(cross * scale * first_scale)

    first_rows(0, BLOCK)
    pl.semaphore_wait(barrier, len(friends))

    def count_copy(i):
        return pltpu.make_async_remote_copy(
            src_ref=count_out,
            dst_ref=count_in.at[i],
            send_sem=count_send,
            recv_sem=count_recv,
            device_id=(slab_at(SLABS[i]), place),
            device_id_type=MESH,
        )

    for i in range(7):
        count_copy(i).start()
    flips_copy.start()
    for k in range(1, CHUNKS):
        land_copy(k).start()
    first_rows(BLOCK, BLOCK)
    first_rows(2 * BLOCK, 2 * BLOCK)

    eye = lax.broadcasted_iota(jnp.int32, (128, 128), 0) == lax.broadcasted_iota(
        jnp.int32, (128, 128), 1
    )
    for row, column in ((in_a, col_a), (in_b, col_b)):
        for i in range(8):
            spread = jnp.where(eye, jnp.broadcast_to(row[i : i + 1], (128, 128)), 0.0)
            column[pl.ds(i * 128, 128), :] = jnp.dot(
                spread.astype(BF16), jnp.ones((128, 128), BF16), preferred_element_type=F32
            )
    flips_copy.wait()
    signs[...] = (2 * flips[...] - 1).astype(F32).astype(BF16)
    settle(count_in, count_send)
    settle(count_in, count_recv)
    count_a, count_b = count_out[0], count_out[1]
    for i in range(7):
        count_a = count_a + count_in[i, 0]
        count_b = count_b + count_in[i, 1]
    balance = jnp.sqrt(count_a * count_b / (count_a + count_b))
    gain_a = (balance / count_a)[0:1]
    gain_b = (balance / count_b)[0:1]
    col_w[...] = col_a[...] * gain_a - col_b[...] * gain_b
    weighted[...] = (kern[...] * wide2(col_w[...])).astype(BF16)
    send_moments(0)
    for k in range(CHUNKS):
        factor_copy(k).start()
        factor_share(k).start()

    def later_chunk(k, _):
        land_copy(k).wait()
        points = point_scale(k)
        cross = lax.dot_general(
            emb[...],
            land[pl.ds(pl.multiple_of(k * CHUNK, CHUNK), CHUNK), :],
            (((1,), (1,)), ((), ())),
            preferred_element_type=F32,
        )
        weighted[...] = (
            jnp.exp2(cross * wide2(row_scale[...]) * points) * wide2(col_w[...])
        ).astype(BF16)
        send_moments(k)

        @pl.when(k >= 2)
        def _():
            sum_slabs(k - 2)

        return 0

    lax.fori_loop(1, CHUNKS, later_chunk, 0)

    sum_slabs(CHUNKS - 2)
    sum_slabs(CHUNKS - 1)
    for n in range(15):
        late_copy(n).start()
    for h in range(2):
        moments[h, core * 8 + slab] = own_sum[h, core]
    settle(factor.at[core], factor_sem)
    settle(factor.at[core], factor_send)
    settle(factor.at[other], factor_recv)

    def wide_copy(t, step):
        chip = chip_at(CHIPS[t]) if t < 7 else y_lo * 4 + x
        return pltpu.make_async_remote_copy(
            src_ref=wide_out.at[t, core_at(step)],
            dst_ref=wide_in.at[core * 8 + t],
            send_sem=wide_send,
            recv_sem=wide_recv,
            device_id=(slab, chip * 2 + core_at(step)),
            device_id_type=MESH,
        )

    def line_copy(t, step):
        return pltpu.make_async_remote_copy(
            src_ref=line_out.at[t, core_at(step)],
            dst_ref=line_in.at[core * 4 + t],
            send_sem=line_send,
            recv_sem=line_recv,
            device_id=(slab, (y_lo * 4 + (x + STEPS[t]) % 4) * 2 + core_at(step)),
            device_id_type=MESH,
        )

    hop = pltpu.make_async_remote_copy(
        src_ref=hop_out,
        dst_ref=hop_in,
        send_sem=hop_send,
        recv_sem=hop_recv,
        device_id=(slab, ((1 - y_lo) * 4 + x) * 2 + core),
        device_id_type=MESH,
    )

    def left_of(h):
        return jnp.concatenate(
            [moments[h, c * 8 : c * 8 + 8].reshape(8 * PART, ROWS) for c in range(2)], axis=1
        )

    def tile(left, chip):
        columns = pl.ds(pl.multiple_of(chip * 256, 256), 256)
        return jnp.dot(
            left,
            jnp.concatenate([factor[0, :, columns], factor[1, :, columns]], axis=0),
            preferred_element_type=F32,
        ).astype(BF16)

    def place_rows(h, c, total):
        for s in range(8):
            wide_rows[pl.ds(s * 64 + c * 32 + h * PART, PART), :] = total[
                s * PART : (s + 1) * PART
            ]

    def early_whiten():
        left = left_of(0)
        for t in range(4):
            for side in range(2):
                value = tile(left, side * 4 + (x + STEPS[t]) % 4)
                line_out[t, 0, side] = value[:, :128]
                line_out[t, 1, side] = value[:, 128:]
            if t < 3:
                line_copy(t, 0).start()
            line_copy(t, 1).start()
        line_in[core * 4 + 3] = line_out[3, core]

    def late_whiten():
        left = left_of(1)
        for t in range(8):
            value = tile(left, chip_at(CHIPS[t]) if t < 7 else y_lo * 4 + x)
            wide_out[t, 0] = value[:, :128]
            wide_out[t, 1] = value[:, 128:]
            if t < 7:
                wide_copy(t, 0).start()
            wide_copy(t, 1).start()
        wide_in[core * 8 + 7] = wide_out[7, core]

    def line_sum(c, side):
        total = line_in[c * 4, side].astype(F32)
        for t in range(1, 4):
            total = total + line_in[c * 4 + t, side].astype(F32)
        return total

    settle(moments.at[0, pl.ds(0, 15)], early_recv)
    early_whiten()
    settle(moments.at[1, pl.ds(0, 15)], late_recv)
    late_whiten()
    settle(line_in.at[pl.ds(0, 7)], line_recv)
    for c in range(2):
        hop_out[c] = line_sum(c, 1 - y_lo).astype(BF16)
    hop.start()
    for c in range(2):
        line_own[c] = line_sum(c, y_lo)
    hop.wait_recv()
    for c in range(2):
        place_rows(0, c, line_own[c] + hop_in[c].astype(F32))
    settle(wide_in.at[pl.ds(0, 15)], wide_recv)
    for c in range(2):
        total = wide_in[c * 8].astype(F32)
        for t in range(1, 8):
            total = total + wide_in[c * 8 + t].astype(F32)
        place_rows(1, c, total)
    values = wide_rows[...]
    norms = lane_sums(values * values)[0:1]
    for i in range(4):
        stat_out[pl.ds(i, 1), :] = norms[:, i * 128 : (i + 1) * 128]
    stat_out[pl.ds(4, 4), :] = jnp.zeros((4, 128), F32)

    pair = pltpu.make_async_remote_copy(
        src_ref=stat_out,
        dst_ref=stat_in,
        send_sem=stat_send,
        recv_sem=stat_recv,
        device_id=(slab, here + other),
        device_id_type=MESH,
    )
    pair.start()
    pair.wait()
    total_in[slab * 8 + y_lo * 4 + x] = stat_out[...] + stat_in[...]

    def total_copy(n):
        slot = slab * 8 + y_lo * 4 + x
        return pltpu.make_async_remote_copy(
            src_ref=total_in.at[slot],
            dst_ref=total_in.at[slot],
            send_sem=total_send,
            recv_sem=total_recv,
            device_id=(slab_at(AROUND[n][0]), chip_at(AROUND[n][1]) * 2 + core),
            device_id_type=MESH,
        )

    for n in range(63):
        total_copy(n).start()
    for i in range(4):
        white_ref[:, pl.ds(i * 128, 128)] = jnp.transpose(
            wide_rows[pl.ds(i * 128, 128), :]
        ).astype(BF16)

    settle(slab_in, slab_send)
    settle(moments.at[0, pl.ds(0, 15)], early_send)
    settle(moments.at[1, pl.ds(0, 15)], late_send)
    settle(wide_in.at[pl.ds(0, 15)], wide_send)
    settle(line_in.at[pl.ds(0, 7)], line_send)
    hop.wait_send()

    settle(total_in.at[pl.ds(0, 63)], total_send)
    settle(total_in.at[pl.ds(0, 63)], total_recv)
    total = total_in[0]
    for i in range(1, 64):
        total = total + total_in[i]
    stat_ref[...] = total


def finish(white_in, stat_in, white_ref, stat_ref):
    white_ref[...] = white_in[...]
    stat_ref[...] = stat_in[0:4] * (1.0 / LANDMARKS)


def local(embeddings, landmarks, factor, flips, labels, counts):
    any_space = pl.BlockSpec(memory_space=pl.ANY)
    vmem = pl.BlockSpec(memory_space=pltpu.VMEM)
    dma = pltpu.SemaphoreType.DMA
    whitened, statistic = pl.pallas_call(
        kernel,
        out_shape=(
            jax.ShapeDtypeStruct((128, 512), BF16),
            jax.ShapeDtypeStruct((8, 128), F32),
        ),
        in_specs=[pl.BlockSpec(memory_space=pltpu.SMEM), vmem] + [any_space] * 4,
        out_specs=(vmem, vmem),
        scratch_shapes=[
            pltpu.VMEM((ROWS, D), BF16),
            pltpu.VMEM((CHUNK * CHUNKS, D), BF16),
            pltpu.VMEM((2, ROWS, 2048), BF16),
            pltpu.VMEM((512, ROWS), jnp.int32),
            pltpu.VMEM((512, ROWS), BF16),
            pltpu.VMEM((ROWS, CHUNK), BF16),
            pltpu.VMEM((ROWS, 128), F32),
            pltpu.VMEM((ROWS, 128), F32),
            pltpu.VMEM((ROWS, 128), F32),
            pltpu.VMEM((ROWS, 128), F32),
            pltpu.VMEM((ROWS, CHUNK), F32),
            pltpu.VMEM((CHUNKS, 512, CHUNK), BF16),
            pltpu.VMEM((CHUNKS, 7, 64, CHUNK), BF16),
            pltpu.VMEM((2, 2, PART, ROWS), BF16),
            pltpu.VMEM((2, 16, PART, ROWS), BF16),
            pltpu.VMEM((8, 2, 8 * PART, 128), BF16),
            pltpu.VMEM((16, 8 * PART, 128), BF16),
            pltpu.VMEM((4, 2, 2, 8 * PART, 128), BF16),
            pltpu.VMEM((8, 2, 8 * PART, 128), BF16),
            pltpu.VMEM((2, 8 * PART, 128), F32),
            pltpu.VMEM((2, 8 * PART, 128), BF16),
            pltpu.VMEM((2, 8 * PART, 128), BF16),
            pltpu.VMEM((512, 128), F32),
            pltpu.VMEM((2, 8, 128), F32),
            pltpu.VMEM((7, 2, 8, 128), F32),
            pltpu.VMEM((8, 128), F32),
            pltpu.VMEM((8, 128), F32),
            pltpu.VMEM((64, 8, 128), F32),
            dma((BLOCKS,)),
            dma((CHUNKS,)),
            dma,
            dma,
            dma,
            dma,
            dma,
            dma,
            dma,
            dma((CHUNKS,)),
            dma,
            dma,
            dma,
            dma,
            dma,
            dma,
            dma,
            dma,
            dma,
            dma,
            dma,
            dma,
            dma,
            dma,
        ],
        compiler_params=pltpu.CompilerParams(
            collective_id=0, has_side_effects=True, vmem_limit_bytes=60 << 20
        ),
    )(counts, labels.reshape(8, 128), embeddings, landmarks, factor, flips)
    whitened, statistic = pl.pallas_call(
        finish,
        out_shape=(
            jax.ShapeDtypeStruct((128, 512), BF16),
            jax.ShapeDtypeStruct((4, 128), F32),
        ),
        in_specs=[vmem, vmem],
        out_specs=(vmem, vmem),
    )(whitened, statistic)
    return whitened, statistic.reshape(512)


def solution(mesh):
    return jax.shard_map(
        local,
        mesh=mesh,
        in_specs=(
            P("sample", None),
            P("landmark", None),
            P("landmark", "sample"),
            P(None, "sample"),
            P("sample"),
            P(),
        ),
        out_specs=(P(("sample", "landmark"), None), P()),
        check_vma=False,
    )
```

```python
import jax
import jax.numpy as jnp
from jax import lax
from jax.experimental import pallas as pl
from jax.experimental.pallas import tpu as pltpu
from jax.sharding import PartitionSpec as P

D = 4096
LANDMARKS = 16384
MESH = pl.DeviceIdType.MESH
F32 = jnp.float32
BF16 = jnp.bfloat16
CHUNK = 256
CHUNKS = 4
ROWS = 1024
BLOCK = 256
BLOCKS = ROWS // BLOCK
PART = 16
STEPS = [2, 1, 3, 0]

SLABS = [(1, 2), (0, 1), (1, 3), (0, 3), (1, 1), (0, 2), (1, 0)]
CHIPS = [(1, 2), (1, 1), (1, 3), (0, 2), (1, 0), (0, 1), (0, 3)]
COLUMN = [(a, b) for a in SLABS + [(0, 0)] for b in (1, 0)][:15]


def kernel(
    counts_ref, labels_ref, emb_hbm, land_hbm, factor_hbm, flips_hbm,
    white_ref, stat_ref,
    emb, land, factor, flips, signs, weighted, row_scale, col_a, col_b, col_w, kern,
    partial_buf, slab_in, own_sum, moments, wide_out, wide_in,
    line_out, line_in, line_own, hop_out, hop_in, wide_rows,
    count_out, count_in, stat_out, stat_in, total_in,
    emb_sem, land_sem, factor_sem, flips_sem,
    factor_send, factor_recv, count_send, count_recv, slab_send, slab_recv,
    early_send, early_recv, late_send, late_recv, wide_send, wide_recv,
    line_send, line_recv, hop_send, hop_recv, stat_send, stat_recv, total_send, total_recv,
):
    slab = lax.axis_index("sample")
    place = lax.axis_index("landmark")
    y_hi, z = slab // 4, slab % 4
    y_lo, x, core = place // 8, (place // 2) % 4, place % 2
    other = (core + 1) % 2

    def slab_at(offset):
        return ((y_hi + offset[0]) % 2) * 4 + (z + offset[1]) % 4

    def chip_at(offset):
        return ((y_lo + offset[0]) % 2) * 4 + (x + offset[1]) % 4

    def core_at(step):
        return (core + step) % 2

    here = (y_lo * 4 + x) * 2

    def settle(like, sem):
        pltpu.make_async_copy(like, like, sem).wait()

    def emb_copy(b):
        rows = pl.ds(b * BLOCK, BLOCK)
        return pltpu.make_async_copy(emb_hbm.at[rows], emb.at[rows], emb_sem.at[b])

    def land_copy(k):
        rows = pl.ds(k * CHUNK, CHUNK)
        return pltpu.make_async_copy(land_hbm.at[rows], land.at[rows], land_sem.at[k])

    def factor_copy(k):
        return pltpu.make_async_copy(
            factor_hbm.at[pl.ds(k * CHUNK, CHUNK)],
            factor.at[core, pl.ds(k * CHUNK, CHUNK)],
            factor_sem,
        )

    def factor_share(k):
        return pltpu.make_async_remote_copy(
            src_ref=factor_hbm.at[pl.ds(k * CHUNK, CHUNK)],
            dst_ref=factor.at[core, pl.ds(k * CHUNK, CHUNK)],
            send_sem=factor_send,
            recv_sem=factor_recv,
            device_id=(slab, here + other),
            device_id_type=MESH,
        )

    flips_copy = pltpu.make_async_copy(flips_hbm, flips, flips_sem)
    land_copy(0).start()
    for b in range(BLOCKS):
        emb_copy(b).start()
    flips_copy.start()

    barrier = pltpu.get_barrier_semaphore()
    friends = [(slab, here + other)]
    for offset in SLABS:
        for step in range(2):
            friends.append((slab_at(offset), here + core_at(step)))
    for offset in CHIPS:
        for step in range(2):
            friends.append((slab, chip_at(offset) * 2 + core_at(step)))
    for offset in COLUMN[:14]:
        if offset[1] == 1:
            friends.append((slab_at(offset[0]), chip_at((1, 0)) * 2 + core))
    for friend in friends:
        pl.semaphore_signal(barrier, inc=1, device_id=friend, device_id_type=MESH)

    own_count = counts_ref[slab]
    corpus = labels_ref[...].astype(F32)
    slot = lax.broadcasted_iota(jnp.int32, (8, 128), 0) * 128 + lax.broadcasted_iota(
        jnp.int32, (8, 128), 1
    )
    live = jnp.where(slot < own_count, 1.0, 0.0).astype(F32)
    in_a, in_b = live * (1.0 - corpus), live * corpus
    count_out[0] = jnp.broadcast_to(jnp.sum(in_a, keepdims=True), (8, 128))
    count_out[1] = jnp.broadcast_to(jnp.sum(in_b, keepdims=True), (8, 128))

    eye = lax.broadcasted_iota(jnp.int32, (128, 128), 0) == lax.broadcasted_iota(
        jnp.int32, (128, 128), 1
    )
    for row, column in ((in_a, col_a), (in_b, col_b)):
        for i in range(8):
            spread = jnp.where(eye, jnp.broadcast_to(row[i : i + 1], (128, 128)), 0.0)
            column[pl.ds(i * 128, 128), :] = jnp.dot(
                spread.astype(BF16), jnp.ones((128, 128), BF16), preferred_element_type=F32
            )
    def squares(ref, start, count):
        total = jnp.zeros((count, 128), F32)
        for t in range(D // 128):
            value = ref[pl.ds(start, count), pl.ds(t * 128, 128)].astype(F32)
            total = total + value * value
        return total

    def lane_sums(value):
        return lax.dot_general(
            jnp.ones((8, 128), F32),
            value,
            (((1,), (1,)), ((), ())),
            precision=lax.Precision.HIGHEST,
            preferred_element_type=F32,
        )

    def point_scale(k):
        parts = []
        for q in range(CHUNK // 64):
            parts.append(squares(land, pl.multiple_of(k * CHUNK + q * 64, 64), 64))
        total = lane_sums(jnp.concatenate(parts, axis=0))
        return lax.rsqrt(total[0:1] * (1.0 / D) + 1e-6)

    def wide2(value):
        return jnp.concatenate([value, value], axis=1)

    fold = 0.5 / 64.0 * 1.4426950408889634

    def slab_copy(k, i):
        there = slab_at(SLABS[i])
        return pltpu.make_async_remote_copy(
            src_ref=partial_buf.at[k, pl.ds(there * 64, 64)],
            dst_ref=slab_in.at[k, i],
            send_sem=slab_send,
            recv_sem=slab_recv.at[k],
            device_id=(there, place),
            device_id_type=MESH,
        )

    def send_moments(k):
        partial_buf[k] = jnp.dot(
            signs[...], weighted[...], preferred_element_type=F32
        ).astype(BF16)
        for i in range(7):
            slab_copy(k, i).start()

    def mom_target(n):
        if n < 14:
            return slab_at(SLABS[n % 7]), n // 7
        return slab, 1

    def early_copy(k, n):
        there, step = mom_target(n)
        columns = pl.ds(k * CHUNK, CHUNK)
        return pltpu.make_async_remote_copy(
            src_ref=own_sum.at[0, core_at(step), :, columns],
            dst_ref=moments.at[0, core * 8 + slab, :, columns],
            send_sem=early_send,
            recv_sem=early_recv,
            device_id=(there, here + core_at(step)),
            device_id_type=MESH,
        )

    def late_copy(n):
        there, step = mom_target(n)
        return pltpu.make_async_remote_copy(
            src_ref=own_sum.at[1, core_at(step)],
            dst_ref=moments.at[1, core * 8 + slab],
            send_sem=late_send,
            recv_sem=late_recv,
            device_id=(there, here + core_at(step)),
            device_id_type=MESH,
        )

    def sum_slabs(k):
        total = partial_buf[k, pl.ds(slab * 64, 64), :].astype(F32)
        settle(slab_in.at[k], slab_recv.at[k])
        for i in range(7):
            total = total + slab_in[k, i].astype(F32)
        total = total.astype(BF16)
        columns = pl.ds(pl.multiple_of(k * CHUNK, CHUNK), CHUNK)
        for c in range(2):
            for h in range(2):
                start = (2 * c + h) * PART
                own_sum[h, c, :, columns] = total[start : start + PART]
        for n in range(15):
            early_copy(k, n).start()

    land_copy(0).wait()
    first_scale = point_scale(0)

    def first_rows(start, count):
        for q in range(count // 64):
            rows = start + q * 64
            total = jnp.sum(squares(emb, rows, 64), axis=1, keepdims=True)
            row_scale[pl.ds(rows, 64), :] = jnp.broadcast_to(
                lax.rsqrt(total * (1.0 / D) + 1e-6) * fold, (64, 128)
            )
        cross = lax.dot_general(
            emb[pl.ds(start, count), :],
            land[0:CHUNK, :],
            (((1,), (1,)), ((), ())),
            preferred_element_type=F32,
        )
        scale = wide2(row_scale[pl.ds(start, count), :])
        kern[pl.ds(start, count), :] = jnp.exp2(cross * scale * first_scale)

    emb_copy(0).wait()
    first_rows(0, BLOCK)
    pl.semaphore_wait(barrier, len(friends))

    def count_copy(i):
        return pltpu.make_async_remote_copy(
            src_ref=count_out,
            dst_ref=count_in.at[i],
            send_sem=count_send,
            recv_sem=count_recv,
            device_id=(slab_at(SLABS[i]), place),
            device_id_type=MESH,
        )

    for i in range(7):
        count_copy(i).start()
    land_copy(1).start()
    emb_copy(1).wait()
    first_rows(BLOCK, BLOCK)
    emb_copy(2).wait()
    emb_copy(3).wait()
    first_rows(2 * BLOCK, 2 * BLOCK)
    for k in range(2, CHUNKS):
        land_copy(k).start()
    flips_copy.wait()
    signs[...] = (2 * flips[...] - 1).astype(F32).astype(BF16)

    settle(count_in, count_send)
    settle(count_in, count_recv)
    count_a, count_b = count_out[0], count_out[1]
    for i in range(7):
        count_a = count_a + count_in[i, 0]
        count_b = count_b + count_in[i, 1]
    balance = jnp.sqrt(count_a * count_b / (count_a + count_b))
    gain_a = (balance / count_a)[0:1]
    gain_b = (balance / count_b)[0:1]
    col_w[...] = col_a[...] * gain_a - col_b[...] * gain_b
    weighted[...] = (kern[...] * wide2(col_w[...])).astype(BF16)
    send_moments(0)
    for k in range(CHUNKS):
        factor_copy(k).start()
        factor_share(k).start()

    def later_chunk(k, _):
        land_copy(k).wait()
        points = point_scale(k)
        cross = lax.dot_general(
            emb[...],
            land[pl.ds(pl.multiple_of(k * CHUNK, CHUNK), CHUNK), :],
            (((1,), (1,)), ((), ())),
            preferred_element_type=F32,
        )
        weighted[...] = (
            jnp.exp2(cross * wide2(row_scale[...]) * points) * wide2(col_w[...])
        ).astype(BF16)
        send_moments(k)

        return 0

    lax.fori_loop(1, CHUNKS, later_chunk, 0)

    for k in range(CHUNKS):
        sum_slabs(k)
    for n in range(15):
        late_copy(n).start()
    for h in range(2):
        moments[h, core * 8 + slab] = own_sum[h, core]
    settle(factor.at[core], factor_sem)
    settle(factor.at[core], factor_send)
    settle(factor.at[other], factor_recv)

    def wide_copy(t, step):
        chip = chip_at(CHIPS[t]) if t < 7 else y_lo * 4 + x
        return pltpu.make_async_remote_copy(
            src_ref=wide_out.at[t, core_at(step)],
            dst_ref=wide_in.at[core * 8 + t],
            send_sem=wide_send,
            recv_sem=wide_recv,
            device_id=(slab, chip * 2 + core_at(step)),
            device_id_type=MESH,
        )

    def line_copy(t, step):
        return pltpu.make_async_remote_copy(
            src_ref=line_out.at[t, core_at(step)],
            dst_ref=line_in.at[core * 4 + t],
            send_sem=line_send,
            recv_sem=line_recv,
            device_id=(slab, (y_lo * 4 + (x + STEPS[t]) % 4) * 2 + core_at(step)),
            device_id_type=MESH,
        )

    hop = pltpu.make_async_remote_copy(
        src_ref=hop_out,
        dst_ref=hop_in,
        send_sem=hop_send,
        recv_sem=hop_recv,
        device_id=(slab, ((1 - y_lo) * 4 + x) * 2 + core),
        device_id_type=MESH,
    )

    def left_of(h):
        return jnp.concatenate(
            [moments[h, c * 8 : c * 8 + 8].reshape(8 * PART, ROWS) for c in range(2)], axis=1
        )

    def tile(left, chip):
        columns = pl.ds(pl.multiple_of(chip * 256, 256), 256)
        return jnp.dot(
            left,
            jnp.concatenate([factor[0, :, columns], factor[1, :, columns]], axis=0),
            preferred_element_type=F32,
        ).astype(BF16)

    def place_rows(h, c, total):
        for s in range(8):
            wide_rows[pl.ds(s * 64 + c * 32 + h * PART, PART), :] = total[
                s * PART : (s + 1) * PART
            ]

    def early_whiten():
        left = left_of(0)
        for t in range(4):
            for side in range(2):
                value = tile(left, side * 4 + (x + STEPS[t]) % 4)
                line_out[t, 0, side] = value[:, :128]
                line_out[t, 1, side] = value[:, 128:]
            if t < 3:
                line_copy(t, 0).start()
            line_copy(t, 1).start()
        line_in[core * 4 + 3] = line_out[3, core]

    def late_whiten():
        left = left_of(1)
        for t in range(8):
            value = tile(left, chip_at(CHIPS[t]) if t < 7 else y_lo * 4 + x)
            wide_out[t, 0] = value[:, :128]
            wide_out[t, 1] = value[:, 128:]
            if t < 7:
                wide_copy(t, 0).start()
            wide_copy(t, 1).start()
        wide_in[core * 8 + 7] = wide_out[7, core]

    def line_sum(c, side):
        total = line_in[c * 4, side].astype(F32)
        for t in range(1, 4):
            total = total + line_in[c * 4 + t, side].astype(F32)
        return total

    settle(moments.at[0, pl.ds(0, 15)], early_recv)
    early_whiten()
    settle(moments.at[1, pl.ds(0, 15)], late_recv)
    late_whiten()
    settle(line_in.at[pl.ds(0, 7)], line_recv)
    for c in range(2):
        hop_out[c] = line_sum(c, 1 - y_lo).astype(BF16)
    hop.start()
    for c in range(2):
        line_own[c] = line_sum(c, y_lo)
    hop.wait_recv()
    for c in range(2):
        place_rows(0, c, line_own[c] + hop_in[c].astype(F32))
    settle(wide_in.at[pl.ds(0, 15)], wide_recv)
    for c in range(2):
        total = wide_in[c * 8].astype(F32)
        for t in range(1, 8):
            total = total + wide_in[c * 8 + t].astype(F32)
        place_rows(1, c, total)
    values = wide_rows[...]
    norms = lane_sums(values * values)[0:1]
    for i in range(4):
        stat_out[pl.ds(i, 1), :] = norms[:, i * 128 : (i + 1) * 128]
    stat_out[pl.ds(4, 4), :] = jnp.zeros((4, 128), F32)

    def stat_copy(n):
        step, turn = (n // 2, n % 2) if n < 6 else (3, 1)
        return pltpu.make_async_remote_copy(
            src_ref=stat_out,
            dst_ref=stat_in.at[x * 2 + core],
            send_sem=stat_send,
            recv_sem=stat_recv,
            device_id=(slab, (y_lo * 4 + (x + STEPS[step]) % 4) * 2 + core_at(turn)),
            device_id_type=MESH,
        )

    for n in range(7):
        stat_copy(n).start()
    stat_in[x * 2 + core] = stat_out[...]
    settle(stat_in.at[pl.ds(0, 7)], stat_recv)
    total = stat_in[0]
    for n in range(1, 8):
        total = total + stat_in[n]
    slot = slab * 2 + y_lo
    total_in[slot] = total

    def total_copy(n):
        offset, side = COLUMN[n]
        return pltpu.make_async_remote_copy(
            src_ref=total_in.at[slot],
            dst_ref=total_in.at[slot],
            send_sem=total_send,
            recv_sem=total_recv,
            device_id=(slab_at(offset), chip_at((side, 0)) * 2 + core),
            device_id_type=MESH,
        )

    for n in range(15):
        total_copy(n).start()
    for i in range(4):
        white_ref[:, pl.ds(i * 128, 128)] = jnp.transpose(
            wide_rows[pl.ds(i * 128, 128), :]
        ).astype(BF16)

    settle(slab_in, slab_send)
    settle(moments.at[0, pl.ds(0, 15)], early_send)
    settle(moments.at[1, pl.ds(0, 15)], late_send)
    settle(wide_in.at[pl.ds(0, 15)], wide_send)
    settle(line_in.at[pl.ds(0, 7)], line_send)
    hop.wait_send()

    settle(stat_in.at[pl.ds(0, 7)], stat_send)
    settle(total_in.at[pl.ds(0, 15)], total_send)
    settle(total_in.at[pl.ds(0, 15)], total_recv)
    total = total_in[0]
    for i in range(1, 16):
        total = total + total_in[i]
    stat_ref[...] = total


def finish(white_in, stat_in, white_ref, stat_ref):
    white_ref[...] = white_in[...]
    stat_ref[...] = stat_in[0:4] * (1.0 / LANDMARKS)


def local(embeddings, landmarks, factor, flips, labels, counts):
    any_space = pl.BlockSpec(memory_space=pl.ANY)
    vmem = pl.BlockSpec(memory_space=pltpu.VMEM)
    dma = pltpu.SemaphoreType.DMA
    whitened, statistic = pl.pallas_call(
        kernel,
        out_shape=(
            jax.ShapeDtypeStruct((128, 512), BF16),
            jax.ShapeDtypeStruct((8, 128), F32),
        ),
        in_specs=[pl.BlockSpec(memory_space=pltpu.SMEM), vmem] + [any_space] * 4,
        out_specs=(vmem, vmem),
        scratch_shapes=[
            pltpu.VMEM((ROWS, D), BF16),
            pltpu.VMEM((CHUNK * CHUNKS, D), BF16),
            pltpu.VMEM((2, ROWS, 2048), BF16),
            pltpu.VMEM((512, ROWS), jnp.int32),
            pltpu.VMEM((512, ROWS), BF16),
            pltpu.VMEM((ROWS, CHUNK), BF16),
            pltpu.VMEM((ROWS, 128), F32),
            pltpu.VMEM((ROWS, 128), F32),
            pltpu.VMEM((ROWS, 128), F32),
            pltpu.VMEM((ROWS, 128), F32),
            pltpu.VMEM((ROWS, CHUNK), F32),
            pltpu.VMEM((CHUNKS, 512, CHUNK), BF16),
            pltpu.VMEM((CHUNKS, 7, 64, CHUNK), BF16),
            pltpu.VMEM((2, 2, PART, ROWS), BF16),
            pltpu.VMEM((2, 16, PART, ROWS), BF16),
            pltpu.VMEM((8, 2, 8 * PART, 128), BF16),
            pltpu.VMEM((16, 8 * PART, 128), BF16),
            pltpu.VMEM((4, 2, 2, 8 * PART, 128), BF16),
            pltpu.VMEM((8, 2, 8 * PART, 128), BF16),
            pltpu.VMEM((2, 8 * PART, 128), F32),
            pltpu.VMEM((2, 8 * PART, 128), BF16),
            pltpu.VMEM((2, 8 * PART, 128), BF16),
            pltpu.VMEM((512, 128), F32),
            pltpu.VMEM((2, 8, 128), F32),
            pltpu.VMEM((7, 2, 8, 128), F32),
            pltpu.VMEM((8, 128), F32),
            pltpu.VMEM((8, 8, 128), F32),
            pltpu.VMEM((16, 8, 128), F32),
            dma((BLOCKS,)),
            dma((CHUNKS,)),
            dma,
            dma,
            dma,
            dma,
            dma,
            dma,
            dma,
            dma((CHUNKS,)),
            dma,
            dma,
            dma,
            dma,
            dma,
            dma,
            dma,
            dma,
            dma,
            dma,
            dma,
            dma,
            dma,
            dma,
        ],
        compiler_params=pltpu.CompilerParams(
            collective_id=0, has_side_effects=True, vmem_limit_bytes=60 << 20
        ),
    )(counts, labels.reshape(8, 128), embeddings, landmarks, factor, flips)
    whitened, statistic = pl.pallas_call(
        finish,
        out_shape=(
            jax.ShapeDtypeStruct((128, 512), BF16),
            jax.ShapeDtypeStruct((4, 128), F32),
        ),
        in_specs=[vmem, vmem],
        out_specs=(vmem, vmem),
    )(whitened, statistic)
    return whitened, statistic.reshape(512)


def solution(mesh):
    return jax.shard_map(
        local,
        mesh=mesh,
        in_specs=(
            P("sample", None),
            P("landmark", None),
            P("landmark", "sample"),
            P(None, "sample"),
            P("sample"),
            P(),
        ),
        out_specs=(P(("sample", "landmark"), None), P()),
        check_vma=False,
    )
```

```python
import jax
import jax.numpy as jnp
from jax import lax
from jax.experimental import pallas as pl
from jax.experimental.pallas import tpu as pltpu
from jax.sharding import PartitionSpec as P

D = 4096
LANDMARKS = 16384
MESH = pl.DeviceIdType.MESH
F32 = jnp.float32
BF16 = jnp.bfloat16
CHUNK = 256
CHUNKS = 4
ROWS = 1024
BLOCK = 256
BLOCKS = ROWS // BLOCK
PART = 16

SLABS = [(1, 2), (1, 1), (1, 3), (0, 2), (1, 0), (0, 1), (0, 3)]
CHIPS = [(1, 2), (1, 1), (1, 3), (0, 2), (1, 0), (0, 1), (0, 3)]
COLUMN = [(a, b) for a in SLABS + [(0, 0)] for b in (1, 0)][:15]
STEPS = [2, 1, 3, 0]


def kernel(
    counts_ref, labels_ref, emb_hbm, land_hbm, factor_hbm, flips_hbm,
    white_ref, stat_ref,
    emb, land, factor, flips, signs, weighted, row_scale, col_a, col_b, col_w, kern,
    partial_buf, slab_in, own_sum, moments, wide_out, wide_in, wide_rows,
    count_out, count_in, stat_out, stat_in, total_in,
    emb_sem, land_sem, factor_sem, flips_sem,
    factor_send, factor_recv, count_send, count_recv, slab_send, slab_recv,
    early_send, early_recv, late_send, late_recv, wide_send, wide_recv, stat_send, stat_recv, total_send, total_recv,
):
    slab = lax.axis_index("sample")
    place = lax.axis_index("landmark")
    y_hi, z = slab // 4, slab % 4
    y_lo, x, core = place // 8, (place // 2) % 4, place % 2
    other = (core + 1) % 2

    def slab_at(offset):
        return ((y_hi + offset[0]) % 2) * 4 + (z + offset[1]) % 4

    def chip_at(offset):
        return ((y_lo + offset[0]) % 2) * 4 + (x + offset[1]) % 4

    def core_at(step):
        return (core + step) % 2

    here = (y_lo * 4 + x) * 2

    def settle(like, sem):
        pltpu.make_async_copy(like, like, sem).wait()

    def emb_copy(b):
        rows = pl.ds(b * BLOCK, BLOCK)
        return pltpu.make_async_copy(emb_hbm.at[rows], emb.at[rows], emb_sem.at[b])

    def land_copy(k):
        rows = pl.ds(k * CHUNK, CHUNK)
        return pltpu.make_async_copy(land_hbm.at[rows], land.at[rows], land_sem.at[k])

    def factor_copy(k):
        return pltpu.make_async_copy(
            factor_hbm.at[pl.ds(k * CHUNK, CHUNK)],
            factor.at[core, pl.ds(k * CHUNK, CHUNK)],
            factor_sem,
        )

    def factor_share(k):
        return pltpu.make_async_remote_copy(
            src_ref=factor_hbm.at[pl.ds(k * CHUNK, CHUNK)],
            dst_ref=factor.at[core, pl.ds(k * CHUNK, CHUNK)],
            send_sem=factor_send,
            recv_sem=factor_recv,
            device_id=(slab, here + other),
            device_id_type=MESH,
        )

    flips_copy = pltpu.make_async_copy(flips_hbm, flips, flips_sem)
    land_copy(0).start()
    for b in range(BLOCKS):
        emb_copy(b).start()

    barrier = pltpu.get_barrier_semaphore()
    friends = [(slab, here + other)]
    for offset in SLABS:
        for step in range(2):
            friends.append((slab_at(offset), here + core_at(step)))
    for offset in CHIPS:
        for step in range(2):
            friends.append((slab, chip_at(offset) * 2 + core_at(step)))
    for offset in COLUMN[:14]:
        if offset[1] == 1:
            friends.append((slab_at(offset[0]), chip_at((1, 0)) * 2 + core))
    for friend in friends:
        pl.semaphore_signal(barrier, inc=1, device_id=friend, device_id_type=MESH)

    own_count = counts_ref[slab]
    corpus = labels_ref[...].astype(F32)
    slot = lax.broadcasted_iota(jnp.int32, (8, 128), 0) * 128 + lax.broadcasted_iota(
        jnp.int32, (8, 128), 1
    )
    live = jnp.where(slot < own_count, 1.0, 0.0).astype(F32)
    in_a, in_b = live * (1.0 - corpus), live * corpus
    count_out[0] = jnp.broadcast_to(jnp.sum(in_a, keepdims=True), (8, 128))
    count_out[1] = jnp.broadcast_to(jnp.sum(in_b, keepdims=True), (8, 128))

    eye = lax.broadcasted_iota(jnp.int32, (128, 128), 0) == lax.broadcasted_iota(
        jnp.int32, (128, 128), 1
    )
    for row, column in ((in_a, col_a), (in_b, col_b)):
        for i in range(8):
            spread = jnp.where(eye, jnp.broadcast_to(row[i : i + 1], (128, 128)), 0.0)
            column[pl.ds(i * 128, 128), :] = jnp.dot(
                spread.astype(BF16), jnp.ones((128, 128), BF16), preferred_element_type=F32
            )
    def squares(ref, start, count):
        total = jnp.zeros((count, 128), F32)
        for t in range(D // 128):
            value = ref[pl.ds(start, count), pl.ds(t * 128, 128)].astype(F32)
            total = total + value * value
        return total

    def lane_sums(value):
        return lax.dot_general(
            jnp.ones((8, 128), F32),
            value,
            (((1,), (1,)), ((), ())),
            precision=lax.Precision.HIGHEST,
            preferred_element_type=F32,
        )

    def point_scale(k):
        parts = []
        for q in range(CHUNK // 64):
            parts.append(squares(land, pl.multiple_of(k * CHUNK + q * 64, 64), 64))
        total = lane_sums(jnp.concatenate(parts, axis=0))
        return lax.rsqrt(total[0:1] * (1.0 / D) + 1e-6)

    def wide2(value):
        return jnp.concatenate([value, value], axis=1)

    fold = 0.5 / 64.0 * 1.4426950408889634

    def slab_copy(k, i):
        there = slab_at(SLABS[i])
        return pltpu.make_async_remote_copy(
            src_ref=partial_buf.at[k, pl.ds(there * 64, 64)],
            dst_ref=slab_in.at[k, i],
            send_sem=slab_send,
            recv_sem=slab_recv.at[k],
            device_id=(there, place),
            device_id_type=MESH,
        )

    def send_moments(k):
        partial_buf[k] = jnp.dot(
            signs[...], weighted[...], preferred_element_type=F32
        ).astype(BF16)
        for i in range(7):
            slab_copy(k, i).start()

    def mom_target(n):
        if n < 14:
            return slab_at(SLABS[n // 2]), n % 2
        return slab, 1

    def early_copy(k, n):
        there, step = mom_target(n)
        columns = pl.ds(k * CHUNK, CHUNK)
        return pltpu.make_async_remote_copy(
            src_ref=own_sum.at[0, core_at(step), :, columns],
            dst_ref=moments.at[0, core * 8 + slab, :, columns],
            send_sem=early_send,
            recv_sem=early_recv,
            device_id=(there, here + core_at(step)),
            device_id_type=MESH,
        )

    def late_copy(n):
        there, step = mom_target(n)
        return pltpu.make_async_remote_copy(
            src_ref=own_sum.at[1, core_at(step)],
            dst_ref=moments.at[1, core * 8 + slab],
            send_sem=late_send,
            recv_sem=late_recv,
            device_id=(there, here + core_at(step)),
            device_id_type=MESH,
        )

    def sum_slabs(k):
        total = partial_buf[k, pl.ds(slab * 64, 64), :].astype(F32)
        settle(slab_in.at[k], slab_recv.at[k])
        for i in range(7):
            total = total + slab_in[k, i].astype(F32)
        total = total.astype(BF16)
        columns = pl.ds(pl.multiple_of(k * CHUNK, CHUNK), CHUNK)
        for c in range(2):
            for h in range(2):
                start = (2 * c + h) * PART
                own_sum[h, c, :, columns] = total[start : start + PART]
        for n in range(15):
            early_copy(k, n).start()

    land_copy(0).wait()
    first_scale = point_scale(0)

    def first_rows(start, count):
        for b in range(start // BLOCK, (start + count) // BLOCK):
            emb_copy(b).wait()
        for q in range(count // 64):
            rows = start + q * 64
            total = jnp.sum(squares(emb, rows, 64), axis=1, keepdims=True)
            row_scale[pl.ds(rows, 64), :] = jnp.broadcast_to(
                lax.rsqrt(total * (1.0 / D) + 1e-6) * fold, (64, 128)
            )
        cross = lax.dot_general(
            emb[pl.ds(start, count), :],
            land[0:CHUNK, :],
            (((1,), (1,)), ((), ())),
            preferred_element_type=F32,
        )
        scale = wide2(row_scale[pl.ds(start, count), :])
        kern[pl.ds(start, count), :] = jnp.exp2(cross * scale * first_scale)

    first_rows(0, BLOCK)
    pl.semaphore_wait(barrier, len(friends))

    def count_copy(i):
        return pltpu.make_async_remote_copy(
            src_ref=count_out,
            dst_ref=count_in.at[i],
            send_sem=count_send,
            recv_sem=count_recv,
            device_id=(slab_at(SLABS[i]), place),
            device_id_type=MESH,
        )

    for i in range(7):
        count_copy(i).start()
    flips_copy.start()
    for k in range(1, CHUNKS):
        land_copy(k).start()
    first_rows(BLOCK, BLOCK)
    first_rows(2 * BLOCK, 2 * BLOCK)

    flips_copy.wait()
    signs[...] = (2 * flips[...] - 1).astype(F32).astype(BF16)
    settle(count_in, count_send)
    settle(count_in, count_recv)
    count_a, count_b = count_out[0], count_out[1]
    for i in range(7):
        count_a = count_a + count_in[i, 0]
        count_b = count_b + count_in[i, 1]
    balance = jnp.sqrt(count_a * count_b / (count_a + count_b))
    gain_a = (balance / count_a)[0:1]
    gain_b = (balance / count_b)[0:1]
    col_w[...] = col_a[...] * gain_a - col_b[...] * gain_b
    weighted[...] = (kern[...] * wide2(col_w[...])).astype(BF16)
    send_moments(0)
    for k in range(CHUNKS):
        factor_copy(k).start()
        factor_share(k).start()

    def later_chunk(k, _):
        land_copy(k).wait()
        points = point_scale(k)
        cross = lax.dot_general(
            emb[...],
            land[pl.ds(pl.multiple_of(k * CHUNK, CHUNK), CHUNK), :],
            (((1,), (1,)), ((), ())),
            preferred_element_type=F32,
        )
        weighted[...] = (
            jnp.exp2(cross * wide2(row_scale[...]) * points) * wide2(col_w[...])
        ).astype(BF16)
        send_moments(k)

        @pl.when(k >= 2)
        def _():
            sum_slabs(k - 2)

        return 0

    lax.fori_loop(1, CHUNKS, later_chunk, 0)

    sum_slabs(CHUNKS - 2)
    sum_slabs(CHUNKS - 1)
    for n in range(15):
        late_copy(n).start()
    for h in range(2):
        moments[h, core * 8 + slab] = own_sum[h, core]
    settle(factor.at[core], factor_sem)
    settle(factor.at[core], factor_send)
    settle(factor.at[other], factor_recv)

    def wide_copy(h, t, step):
        chip = chip_at(CHIPS[t]) if t < 7 else y_lo * 4 + x
        return pltpu.make_async_remote_copy(
            src_ref=wide_out.at[h, t, core_at(step)],
            dst_ref=wide_in.at[h, core * 8 + t],
            send_sem=wide_send,
            recv_sem=wide_recv.at[h],
            device_id=(slab, chip * 2 + core_at(step)),
            device_id_type=MESH,
        )

    def whiten(h):
        left = jnp.concatenate(
            [moments[h, c * 8 : c * 8 + 8].reshape(8 * PART, ROWS) for c in range(2)], axis=1
        )
        for t in range(8):
            q = chip_at(CHIPS[t]) if t < 7 else y_lo * 4 + x
            columns = pl.ds(pl.multiple_of(q * 256, 256), 256)
            value = jnp.dot(
                left,
                jnp.concatenate([factor[0, :, columns], factor[1, :, columns]], axis=0),
                preferred_element_type=F32,
            ).astype(BF16)
            wide_out[h, t, 0] = value[:, :128]
            wide_out[h, t, 1] = value[:, 128:]
            if t < 7:
                wide_copy(h, t, 0).start()
            wide_copy(h, t, 1).start()
        wide_in[h, core * 8 + 7] = wide_out[h, 7, core]

    def gather(h):
        settle(wide_in.at[h, pl.ds(0, 15)], wide_recv.at[h])
        for c in range(2):
            total = wide_in[h, c * 8].astype(F32)
            for t in range(1, 8):
                total = total + wide_in[h, c * 8 + t].astype(F32)
            for s in range(8):
                wide_rows[pl.ds(s * 64 + c * 32 + h * PART, PART), :] = total[
                    s * PART : (s + 1) * PART
                ]

    settle(moments.at[0, pl.ds(0, 15)], early_recv)
    whiten(0)
    settle(moments.at[1, pl.ds(0, 15)], late_recv)
    whiten(1)
    gather(0)
    gather(1)
    values = wide_rows[...]
    norms = lane_sums(values * values)[0:1]
    for i in range(4):
        stat_out[pl.ds(i, 1), :] = norms[:, i * 128 : (i + 1) * 128]
    stat_out[pl.ds(4, 4), :] = jnp.zeros((4, 128), F32)

    def stat_copy(n):
        step, turn = (n // 2, n % 2) if n < 6 else (3, 1)
        return pltpu.make_async_remote_copy(
            src_ref=stat_out,
            dst_ref=stat_in.at[x * 2 + core],
            send_sem=stat_send,
            recv_sem=stat_recv,
            device_id=(slab, (y_lo * 4 + (x + STEPS[step]) % 4) * 2 + core_at(turn)),
            device_id_type=MESH,
        )

    for n in range(7):
        stat_copy(n).start()
    stat_in[x * 2 + core] = stat_out[...]
    settle(stat_in.at[pl.ds(0, 7)], stat_recv)
    total = stat_in[0]
    for n in range(1, 8):
        total = total + stat_in[n]
    slot = slab * 2 + y_lo
    total_in[slot] = total

    def total_copy(n):
        offset, side = COLUMN[n]
        return pltpu.make_async_remote_copy(
            src_ref=total_in.at[slot],
            dst_ref=total_in.at[slot],
            send_sem=total_send,
            recv_sem=total_recv,
            device_id=(slab_at(offset), chip_at((side, 0)) * 2 + core),
            device_id_type=MESH,
        )

    for n in range(15):
        total_copy(n).start()
    for i in range(4):
        white_ref[:, pl.ds(i * 128, 128)] = jnp.transpose(
            wide_rows[pl.ds(i * 128, 128), :]
        ).astype(BF16)

    settle(slab_in, slab_send)
    settle(moments.at[0, pl.ds(0, 15)], early_send)
    settle(moments.at[1, pl.ds(0, 15)], late_send)
    settle(wide_in.at[:, pl.ds(0, 15)], wide_send)
    settle(stat_in.at[pl.ds(0, 7)], stat_send)

    settle(total_in.at[pl.ds(0, 15)], total_send)
    settle(total_in.at[pl.ds(0, 15)], total_recv)
    total = total_in[0]
    for i in range(1, 16):
        total = total + total_in[i]
    stat_ref[...] = total


def finish(white_in, stat_in, white_ref, stat_ref):
    white_ref[...] = white_in[...]
    stat_ref[...] = stat_in[0:4] * (1.0 / LANDMARKS)


def local(embeddings, landmarks, factor, flips, labels, counts):
    any_space = pl.BlockSpec(memory_space=pl.ANY)
    vmem = pl.BlockSpec(memory_space=pltpu.VMEM)
    dma = pltpu.SemaphoreType.DMA
    whitened, statistic = pl.pallas_call(
        kernel,
        out_shape=(
            jax.ShapeDtypeStruct((128, 512), BF16),
            jax.ShapeDtypeStruct((8, 128), F32),
        ),
        in_specs=[pl.BlockSpec(memory_space=pltpu.SMEM), vmem] + [any_space] * 4,
        out_specs=(vmem, vmem),
        scratch_shapes=[
            pltpu.VMEM((ROWS, D), BF16),
            pltpu.VMEM((CHUNK * CHUNKS, D), BF16),
            pltpu.VMEM((2, ROWS, 2048), BF16),
            pltpu.VMEM((512, ROWS), jnp.int32),
            pltpu.VMEM((512, ROWS), BF16),
            pltpu.VMEM((ROWS, CHUNK), BF16),
            pltpu.VMEM((ROWS, 128), F32),
            pltpu.VMEM((ROWS, 128), F32),
            pltpu.VMEM((ROWS, 128), F32),
            pltpu.VMEM((ROWS, 128), F32),
            pltpu.VMEM((ROWS, CHUNK), F32),
            pltpu.VMEM((CHUNKS, 512, CHUNK), BF16),
            pltpu.VMEM((CHUNKS, 7, 64, CHUNK), BF16),
            pltpu.VMEM((2, 2, PART, ROWS), BF16),
            pltpu.VMEM((2, 16, PART, ROWS), BF16),
            pltpu.VMEM((2, 8, 2, 8 * PART, 128), BF16),
            pltpu.VMEM((2, 16, 8 * PART, 128), BF16),
            pltpu.VMEM((512, 128), F32),
            pltpu.VMEM((2, 8, 128), F32),
            pltpu.VMEM((7, 2, 8, 128), F32),
            pltpu.VMEM((8, 128), F32),
            pltpu.VMEM((8, 8, 128), F32),
            pltpu.VMEM((16, 8, 128), F32),
            dma((BLOCKS,)),
            dma((CHUNKS,)),
            dma,
            dma,
            dma,
            dma,
            dma,
            dma,
            dma,
            dma((CHUNKS,)),
            dma,
            dma,
            dma,
            dma,
            dma,
            dma((2,)),
            dma,
            dma,
            dma,
            dma,
        ],
        compiler_params=pltpu.CompilerParams(
            collective_id=0, has_side_effects=True, vmem_limit_bytes=60 << 20
        ),
    )(counts, labels.reshape(8, 128), embeddings, landmarks, factor, flips)
    whitened, statistic = pl.pallas_call(
        finish,
        out_shape=(
            jax.ShapeDtypeStruct((128, 512), BF16),
            jax.ShapeDtypeStruct((4, 128), F32),
        ),
        in_specs=[vmem, vmem],
        out_specs=(vmem, vmem),
    )(whitened, statistic)
    return whitened, statistic.reshape(512)


def solution(mesh):
    return jax.shard_map(
        local,
        mesh=mesh,
        in_specs=(
            P("sample", None),
            P("landmark", None),
            P("landmark", "sample"),
            P(None, "sample"),
            P("sample"),
            P(),
        ),
        out_specs=(P(("sample", "landmark"), None), P()),
        check_vma=False,
    )
```
